256 devices in a mesh: row: 16 (over x_hi, y, core), col: 16 (over z, x_lo).
Axes of the slice: x: 4 (x_hi: 2, x_lo: 2; x = x_hi * 2 + x_lo), y: 4, z: 8, core: 2. Of those that a mesh axis runs over, the one named last changes fastest.
Arguments:
- item_features: bfloat16 [131072, 256], P(('row', 'col')), may hold values from -6 to 6
- self_weight: bfloat16 [256, 256], replicated, may hold values from -0.375 to 0.375
- neighbor_weight: bfloat16 [256, 256], replicated, may hold values from -0.375 to 0.375
- layer_bias: float32 [256], replicated, may hold values from -3 to 3
- norm_gain: float32 [256], replicated, may hold values from 0.5 to 1.5
- blocks: bfloat16 [16, 16, 256, 128, 128], P('row', 'col'), may hold values from 0 to 0.0625
- block_rows: int32 [16, 16, 256], P('row', 'col'), may hold values from 0 to 63, as said below
- block_cols: int32 [16, 16, 256], P('row', 'col'), may hold values from 0 to 63, as said below
- counts: int32 [16, 16], P('row', 'col'), may hold values from 1 to 256, as said below
- queries: bfloat16 [4096, 256], P(('row', 'col')), may hold values from -6 to 6
- candidates: int32 [4096, 64], P(('row', 'col')), may hold values from 0 to 131071, as said below
- positions: int32 [4096, 64], P(('row', 'col')), may hold values from 0 to 63, each once within a row
- position_table: float32 [64, 128], replicated, may hold values from -6 to 6
- tower_weight: float32 [128], replicated, may hold values from -0.5 to 0.5
- score_cotangent: bfloat16 [4096, 64], P(('row', 'col')), may hold values from -6 to 6
Outputs:
- hidden: bfloat16 [131072, 256], P(('row', 'col'))
- scores: float32 [4096, 64], P(('row', 'col'))
- item_grads: float32 [131072, 256], P(('row', 'col'))
The draws below stay inside these ranges and needn't reach their ends.
Inputs may be any that keep to these rules, and one draw needn't show every extreme that they name: Slots s >= counts[r, c] are not part of A. In every draw all devices of some row have 256 live slots. `block_rows`: the live slots of one device name distinct pairs of block row and block column. `block_cols`: the live slots of one device name distinct pairs of block row and block column. The candidates of requests of piece p (rows p * 16 to (p + 1) * 16 - 1) are items of column set p % 16; an item may appear several times.
All inputs are finite; a program needn't handle non-finite values.
Results may differ from the reference program's by a relative error of at most 0.04.
Values may be sent and summed in bfloat16 or wider, within the bound.
No kernel may reach another device: no remote copies, remote signals or barrier semaphores. Data moves between devices by JAX's collectives and lax.ppermute only.
A program may use at most 128 MiB of HBM per device.

```python
import jax
import jax.numpy as jnp
from jax import lax

D = 256
POS_WIDTH = 128
BLK = 128
CANDS = 64
ITEMS_DEV = 512
BLOCKS_DEV = 256
REQ_DEV = 16
ITEMS = 131072
REQS = 4096
N_ROW = 16
N_COL = 16


def layout_draw(key):
    row_blocks = N_COL * ITEMS_DEV // BLK
    col_blocks = N_ROW * ITEMS_DEV // BLK
    position_total = row_blocks * col_blocks
    base_key = jax.random.fold_in(key, 11)
    busy_key, spread_key, place_key = jax.random.split(base_key, 3)
    busy_row = jax.random.randint(busy_key, (), 0, N_ROW)
    spread = jax.random.randint(spread_key, (N_ROW, N_COL), max(BLOCKS_DEV // 8, 1), BLOCKS_DEV // 2 + 1)
    counts = jnp.where(jnp.arange(N_ROW)[:, None] == busy_row, BLOCKS_DEV, spread).astype(jnp.int32)
    device_keys = jax.random.split(place_key, N_ROW * N_COL)

    def one_device(subkey, device_count):
        shuffled = jax.random.permutation(subkey, position_total)[:BLOCKS_DEV]
        slot_index = jnp.arange(BLOCKS_DEV)
        ordered = jnp.sort(jnp.where(slot_index < device_count, shuffled, position_total + shuffled))
        return ordered % position_total
    placed = jax.vmap(one_device)(device_keys, counts.reshape(-1)).reshape(N_ROW, N_COL, BLOCKS_DEV)
    return (counts, (placed // col_blocks).astype(jnp.int32), (placed % col_blocks).astype(jnp.int32))


def draw_counts(key, part):
    return layout_draw(key)[0]


def draw_block_rows(key, part):
    return layout_draw(key)[1]


def draw_block_cols(key, part):
    return layout_draw(key)[2]


def draw_candidates(key, part):
    subkey = jax.random.fold_in(key, 23)
    device_total = N_ROW * N_COL
    local_rows = jax.random.randint(subkey, (device_total, REQ_DEV, CANDS), 0, N_ROW * ITEMS_DEV)
    column = (jnp.arange(device_total) % N_COL)[:, None, None]
    owner_row = local_rows // ITEMS_DEV
    item_ids = (owner_row * N_COL + column) * ITEMS_DEV + local_rows % ITEMS_DEV
    item_ids = item_ids.reshape(REQS, CANDS)
    item_ids = item_ids.at[0, 0].set(0)
    item_ids = item_ids.at[REQS - 1, 0].set(ITEMS - 1)
    return item_ids.astype(jnp.int32)


def levels(own_key, shape, shards, low, top_value):
    gain = 1.0
    for position, shards_of in shards:
        heights = jax.random.uniform(jax.random.fold_in(jax.random.fold_in(own_key, 6), position), (shards_of,), jnp.float32, low / len(shards), top_value / len(shards))
        gain = gain * jnp.repeat(jnp.exp(heights), shape[position] // shards_of).reshape((-1,) + (1,) * (len(shape) - 1 - position))
    return gain


def bell_draw(own_key, dims, scale, bound, pieces=(), kind=jnp.bfloat16):
    array = jax.random.normal(own_key, dims, jnp.float32) * scale
    if len(pieces) > 0:
        array = levels(own_key, dims, pieces, -0.22, 0.18) * array
    return jnp.clip(array, min=-bound, max=bound).astype(kind)


def setup_inputs(seed: int = 0) -> dict:
    arg_keys = jax.random.split(jax.random.key(seed), 16)
    return {
        "item_features": bell_draw(arg_keys[0], (ITEMS, D), 1.0, 6.0, ((0, 256),)),
        "self_weight": bell_draw(arg_keys[1], (D, D), D ** -0.5, 0.375),
        "neighbor_weight": bell_draw(arg_keys[2], (D, D), D ** -0.5, 0.375),
        "layer_bias": bell_draw(arg_keys[3], (D,), 0.5, 3.0, (), jnp.float32),
        "norm_gain": jnp.clip(1.0 + 0.1 * jax.random.normal(arg_keys[4], (D,), jnp.float32), 0.5, 1.5),
        "blocks": jnp.clip(0.0625 * jax.random.uniform(arg_keys[5], (N_ROW, N_COL, BLOCKS_DEV, BLK, BLK), jnp.float32) ** levels(arg_keys[5], (N_ROW, N_COL, BLOCKS_DEV, BLK, BLK), ((0, 16), (1, 16)), -0.2, 0.2), 0.0, 0.0625).astype(jnp.bfloat16),
        "block_rows": draw_block_rows(jax.random.fold_in(arg_keys[15], 71), 0),
        "block_cols": draw_block_cols(jax.random.fold_in(arg_keys[15], 71), 0),
        "counts": draw_counts(jax.random.fold_in(arg_keys[15], 71), 0),
        "queries": bell_draw(arg_keys[9], (REQS, D), 1.0, 6.0, ((0, 256),)),
        "candidates": draw_candidates(jax.random.fold_in(arg_keys[15], 71), 0),
        "positions": jax.vmap(lambda own: jax.random.permutation(own, CANDS))(jax.random.split(arg_keys[11], REQS)).reshape((REQS, CANDS)).astype(jnp.int32),
        "position_table": bell_draw(arg_keys[12], (CANDS, POS_WIDTH), 1.0, 6.0, (), jnp.float32),
        "tower_weight": bell_draw(arg_keys[13], (POS_WIDTH,), POS_WIDTH ** -0.5, 0.5, (), jnp.float32),
        "score_cotangent": bell_draw(arg_keys[14], (REQS, CANDS), 1.0, 6.0, ((0, 256),)),
    }


norm_eps = 1e-05

def normalize(preact, norm_gain):
    active = jax.nn.silu(preact)
    return norm_gain * active * lax.rsqrt(lax.optimization_barrier(jnp.mean(active * active, axis=-1, keepdims=True)) + norm_eps)

def round_part(value):
    return lax.optimization_barrier(value.astype(jnp.bfloat16)).astype(jnp.float32)

def reference(item_features, self_weight, neighbor_weight, layer_bias, norm_gain, blocks, block_rows, block_cols, counts, queries, candidates, positions, position_table, tower_weight, score_cotangent):
    row_blocks = N_COL * ITEMS_DEV // BLK
    col_blocks = N_ROW * ITEMS_DEV // BLK
    item_grid = item_features.reshape(N_ROW, N_COL, ITEMS_DEV, D)
    slot_index = jnp.arange(BLOCKS_DEV)

    def forward_row(row_index):

        def add_column(col_index, summed):
            source = lax.dynamic_index_in_dim(item_grid, col_index, 1, False).reshape(col_blocks, BLK, D)
            tile_set = blocks[row_index, col_index].astype(jnp.float32)
            is_live = (slot_index < counts[row_index, col_index]).astype(jnp.float32)
            gathered = source[block_cols[row_index, col_index]].astype(jnp.float32)
            product = jnp.einsum('nij,njd->nid', tile_set, gathered) * is_live[:, None, None]
            return summed + round_part(jax.ops.segment_sum(product, block_rows[row_index, col_index], row_blocks))
        return lax.fori_loop(0, N_COL, add_column, jnp.zeros((row_blocks, BLK, D), jnp.float32))
    aggregate = lax.map(forward_row, jnp.arange(N_ROW)).reshape(ITEMS, D)
    preact = jnp.dot(item_features, self_weight, preferred_element_type=jnp.float32)
    preact = preact + jnp.dot(aggregate.astype(jnp.bfloat16), neighbor_weight, preferred_element_type=jnp.float32) + layer_bias
    normed, pullback = jax.vjp(lambda value: normalize(value, norm_gain), preact)
    hidden = normed.astype(jnp.bfloat16)
    score_scale = D ** (-0.5)
    tower_values = lax.optimization_barrier(jnp.sum(jax.nn.relu(position_table) * tower_weight, axis=-1))
    device_total = N_ROW * N_COL
    cand_dev = candidates.reshape(device_total, REQ_DEV, CANDS)
    query_dev = queries.reshape(device_total, REQ_DEV, D)
    cot_dev = score_cotangent.reshape(device_total, REQ_DEV, CANDS)

    def score_device(pair):
        ids, query_rows = pair
        picked = hidden[ids].astype(jnp.float32)
        return lax.optimization_barrier(jnp.sum(picked * query_rows.astype(jnp.float32)[:, None, :], axis=-1))
    raw_scores = lax.map(score_device, (cand_dev, query_dev)).reshape(REQS, CANDS)
    scores = raw_scores * score_scale + tower_values[positions]

    def add_grads(device, summed):
        ids = lax.dynamic_index_in_dim(cand_dev, device, 0, False)
        query_rows = lax.dynamic_index_in_dim(query_dev, device, 0, False).astype(jnp.float32)
        cot_rows = lax.dynamic_index_in_dim(cot_dev, device, 0, False).astype(jnp.float32)
        terms = (cot_rows[:, :, None] * query_rows[:, None, :]).reshape(-1, D)
        return summed.at[ids.reshape(-1)].add(terms)
    grad_hidden = lax.fori_loop(0, device_total, add_grads, jnp.zeros((ITEMS, D), jnp.float32)) * score_scale
    grad_preact = pullback(grad_hidden)[0]
    grad_rounded = grad_preact.astype(jnp.bfloat16)
    grad_self = jnp.dot(grad_rounded, self_weight.T, preferred_element_type=jnp.float32)
    back_source = jnp.dot(grad_rounded, neighbor_weight.T, preferred_element_type=jnp.float32).astype(jnp.bfloat16)
    back_grid = back_source.reshape(N_ROW, row_blocks, BLK, D)

    def backward_column(col_index):

        def add_row(row_index, summed):
            source = lax.dynamic_index_in_dim(back_grid, row_index, 0, False)
            tile_set = blocks[row_index, col_index].astype(jnp.float32)
            is_live = (slot_index < counts[row_index, col_index]).astype(jnp.float32)
            gathered = source[block_rows[row_index, col_index]].astype(jnp.float32)
            product = jnp.einsum('nij,nid->njd', tile_set, gathered) * is_live[:, None, None]
            return summed + round_part(jax.ops.segment_sum(product, block_cols[row_index, col_index], col_blocks))
        return lax.fori_loop(0, N_ROW, add_row, jnp.zeros((col_blocks, BLK, D), jnp.float32))
    back_sum = lax.map(backward_column, jnp.arange(N_COL)).reshape(N_COL, N_ROW, ITEMS_DEV, D)
    back_sum = back_sum.transpose(1, 0, 2, 3).reshape(ITEMS, D)
    return (hidden, scores, grad_self + back_sum)
```

```python
import functools

import jax
import jax.numpy as jnp
from jax import lax
from jax.experimental import pallas as pl
from jax.experimental.pallas import tpu as pltpu
from jax.sharding import Mesh
from jax.sharding import PartitionSpec as P

ROW = ("xh", "y", "core")
COL = ("z", "xl")
ALL = ROW + COL
CHIP = ("xh", "y")
XH, Y = 2, 4
NORM_EPS = 1e-05


def products_kernel(
    n_pieces, n_outs, piece_rows, transpose, group, unroll,
    tgt, src, cnt, in_pos, out_pos, blk, *rest,
):
    pieces, rest = rest[:n_pieces], rest[n_pieces:]
    outs, (source, acc, sems) = rest[:n_outs], rest[n_outs:]
    g = pl.program_id(0)

    @pl.when(g == 0)
    def _():
        copies = []
        for i in range(n_pieces):
            at = pl.multiple_of(in_pos[i] * piece_rows, piece_rows)
            copies.append(
                pltpu.make_async_copy(
                    pieces[i].at[pl.ds(0, piece_rows), :],
                    source.at[pl.ds(at, piece_rows), :],
                    sems.at[i],
                )
            )
        for copy in copies:
            copy.start()
        acc[...] = jnp.zeros_like(acc)
        for copy in copies:
            copy.wait()

    live = jnp.clip(cnt[0] - g * group, 0, group)
    dims = (((0,), (0,)), ((), ())) if transpose else (((1,), (0,)), ((), ()))

    def one(k):
        s = g * group + k
        to = pl.multiple_of(tgt[s] * 128, 128)
        at = pl.multiple_of(src[s] * 128, 128)
        acc[pl.ds(to, 128), :] += lax.dot_general(
            blk[k], source[pl.ds(at, 128), :], dims, preferred_element_type=jnp.float32
        )

    def some(q, carry):
        for u in range(unroll):
            one(q * unroll + u)
        return carry

    def single(k, carry):
        one(k)
        return carry

    whole = live // unroll
    lax.fori_loop(0, whole, some, 0)
    lax.fori_loop(whole * unroll, live, single, 0)

    @pl.when(g == pl.num_programs(0) - 1)
    def _():
        slot = 0
        for out in outs:
            for j in range(out.shape[0] // 512):
                at = pl.multiple_of(out_pos[slot] * 512, 512)
                out[pl.ds(j * 512, 512), :] = acc[pl.ds(at, 512), :].astype(out.dtype)
                slot += 1


def block_products(
    tiles, targets, sources, count, pieces, in_pos, piece_rows, out_sizes, out_pos, transpose,
    group=32, unroll=8,
):
    slots, size, _ = tiles.shape
    width = pieces[0].shape[1]
    rows = piece_rows * len(pieces)

    def tile_map(g, tgt, src, cnt, *_):
        return (jnp.minimum(g, (cnt[0] - 1) // group), 0, 0)

    def whole(g, *_):
        return (0, 0)

    out_rows = sum(out_sizes)
    return pl.pallas_call(
        functools.partial(
            products_kernel, len(pieces), len(out_sizes), piece_rows, transpose, group, unroll
        ),
        out_shape=[jax.ShapeDtypeStruct((n, width), jnp.bfloat16) for n in out_sizes],
        grid_spec=pltpu.PrefetchScalarGridSpec(
            num_scalar_prefetch=5,
            grid=(slots // group,),
            in_specs=[pl.BlockSpec((group, size, size), tile_map)]
            + [pl.BlockSpec(memory_space=pl.ANY)] * len(pieces),
            out_specs=[
                pl.BlockSpec((n, width), whole, pipeline_mode=pl.Buffered(1)) for n in out_sizes
            ],
            scratch_shapes=[
                pltpu.VMEM((rows, width), jnp.bfloat16),
                pltpu.VMEM((out_rows, width), jnp.float32),
                pltpu.SemaphoreType.DMA((len(pieces),)),
            ],
        ),
        compiler_params=pltpu.CompilerParams(
            dimension_semantics=("arbitrary",), vmem_limit_bytes=40 << 20
        ),
        cost_estimate=pl.CostEstimate(
            flops=2 * slots * size * size * width,
            bytes_accessed=2 * (slots * size * size + rows * width + out_rows * width),
            transcendentals=0,
        ),
        name="products",
    )(targets, sources, count, in_pos, out_pos, tiles, *pieces)


def weights_kernel(n_pieces, at_row, in_pos, base, *rest):
    pieces, (weights, lids, queries, packed, sems) = rest[:n_pieces], rest[n_pieces:]
    copies = []
    for i in range(n_pieces):
        p = in_pos[i]
        copies.append(
            pltpu.make_async_copy(
                pieces[i].at[pl.ds(at_row, 32), :], packed.at[p], sems.at[i]
            )
        )
    for copy in copies:
        copy.start()
    for copy in copies:
        copy.wait()
    whole = packed[...]
    queries[...] = whole[:, :16, :].reshape(queries.shape)
    meta = whole[:, 16:, :].reshape(queries.shape).astype(jnp.float32).T
    lid = meta[0:64] * 128.0 + meta[64:128] - base[0].astype(jnp.float32) * 512.0
    cot = meta[128:192]
    lids[0:64, :] = lid
    lids[64:128, :] = cot
    step = 64
    rows = lax.broadcasted_iota(jnp.int32, (step, 256), 0).astype(jnp.float32)

    def chunk(c, carry):
        item = rows + (c * step).astype(jnp.float32)

        def add(k, total):
            return total + jnp.where(
                item == lids[pl.ds(k, 1), :], lids[pl.ds(64 + k, 1), :], 0.0
            )

        total = lax.fori_loop(0, 64, add, jnp.zeros((step, 256), jnp.float32), unroll=8)
        weights[pl.ds(pl.multiple_of(c * step, step), step), :] = total
        return carry

    lax.fori_loop(0, 512 // step, chunk, 0)


def request_weights(pieces, in_pos, my_row, at_row):
    n = len(pieces)
    return pl.pallas_call(
        functools.partial(weights_kernel, n, at_row),
        out_shape=[
            jax.ShapeDtypeStruct((512, 256), jnp.float32),
            jax.ShapeDtypeStruct((128, 256), jnp.float32),
            jax.ShapeDtypeStruct((256, 256), jnp.bfloat16),
        ],
        grid_spec=pltpu.PrefetchScalarGridSpec(
            num_scalar_prefetch=2,
            grid=(1,),
            in_specs=[pl.BlockSpec(memory_space=pl.ANY)] * n,
            out_specs=[
                pl.BlockSpec((512, 256), lambda g, *_: (0, 0)),
                pl.BlockSpec((128, 256), lambda g, *_: (0, 0)),
                pl.BlockSpec((256, 256), lambda g, *_: (0, 0)),
            ],
            scratch_shapes=[
                pltpu.VMEM((n, 32, 256), jnp.bfloat16),
                pltpu.SemaphoreType.DMA((n,)),
            ],
        ),
        compiler_params=pltpu.CompilerParams(vmem_limit_bytes=16 << 20),
        cost_estimate=pl.CostEstimate(
            flops=4 * 64 * 512 * 256, bytes_accessed=1 << 20, transcendentals=0
        ),
        name="weights",
    )(in_pos, my_row, *pieces)


def layer_kernel(
    items, agg, self_w, neigh_w, bias, gain, weights, queries, hidden, back, grad_self
):
    pre = jnp.dot(items[...], self_w[...], preferred_element_type=jnp.float32)
    pre = pre + jnp.dot(agg[...], neigh_w[...], preferred_element_type=jnp.float32) + bias[...]
    gate = jax.nn.sigmoid(pre)
    act = pre * gate
    width = act.shape[1]
    inv = lax.rsqrt(jnp.sum(act * act, axis=1, keepdims=True) * (1.0 / width) + NORM_EPS)
    scale = gain[...]
    hidden[...] = (scale * act * inv).astype(hidden.dtype)
    w = weights[...]
    high = w.astype(jnp.bfloat16)
    low = (w - high.astype(jnp.float32)).astype(jnp.bfloat16)
    q = queries[...]
    grad = jnp.dot(high, q, preferred_element_type=jnp.float32)
    grad = grad + jnp.dot(low, q, preferred_element_type=jnp.float32)
    grad = grad * (scale * (width**-0.5))
    mean = jnp.sum(grad * act, axis=1, keepdims=True) * (1.0 / width)
    d_act = inv * (grad - act * (inv * inv * mean))
    d_pre = (d_act * (gate * (1.0 + pre * (1.0 - gate)))).astype(jnp.bfloat16)
    last = (((1,), (1,)), ((), ()))
    back[...] = lax.dot_general(
        d_pre, neigh_w[...], last, preferred_element_type=jnp.float32
    ).astype(back.dtype)
    grad_self[...] = lax.dot_general(d_pre, self_w[...], last, preferred_element_type=jnp.float32)


def layer(items, agg, self_w, neigh_w, bias, gain, weights, queries):
    rows, width = items.shape
    step = 128
    tile = pl.BlockSpec((step, width), lambda g: (g, 0))

    def fixed(shape):
        return pl.BlockSpec(shape, lambda g: (0, 0))

    return pl.pallas_call(
        layer_kernel,
        out_shape=[
            jax.ShapeDtypeStruct((rows, width), jnp.bfloat16),
            jax.ShapeDtypeStruct((rows, width), jnp.bfloat16),
            jax.ShapeDtypeStruct((rows, width), jnp.float32),
        ],
        grid=(rows // step,),
        in_specs=[
            tile, tile, fixed((width, width)), fixed((width, width)), fixed((1, width)),
            fixed((1, width)), tile, fixed((256, width)),
        ],
        out_specs=[tile, tile, tile],
        compiler_params=pltpu.CompilerParams(vmem_limit_bytes=16 << 20),
        cost_estimate=pl.CostEstimate(
            flops=12 * rows * width * width, bytes_accessed=2 << 20, transcendentals=rows * width
        ),
        name="layer",
    )(items, agg, self_w, neigh_w, bias, gain, weights, queries)


def scores_kernel(hidden, queries, lids, out, table, picked):
    table[...] = lax.dot_general(
        hidden[...], queries[...], (((1,), (1,)), ((), ())), preferred_element_type=jnp.float32
    )
    rows = lax.broadcasted_iota(jnp.int32, (8, 256), 0).astype(jnp.float32)

    def pick(k, carry):
        lid = jnp.broadcast_to(lids[pl.ds(k, 1), :], (8, 256)) - rows
        total = jnp.zeros((8, 256), jnp.float32)
        for j in range(64):
            total = total + jnp.where(lid == 8.0 * j, table[8 * j : 8 * j + 8, :], 0.0)
        picked[pl.ds(k, 1), :] = jnp.sum(total, axis=0, keepdims=True)
        return carry

    lax.fori_loop(0, 64, pick, 0)
    out[...] = picked[...].T


def owner_scores(hidden, queries, lids):
    return pl.pallas_call(
        scores_kernel,
        out_shape=jax.ShapeDtypeStruct((256, 64), jnp.float32),
        scratch_shapes=[
            pltpu.VMEM((512, 256), jnp.float32),
            pltpu.VMEM((64, 256), jnp.float32),
        ],
        compiler_params=pltpu.CompilerParams(vmem_limit_bytes=16 << 20),
        cost_estimate=pl.CostEstimate(
            flops=4 * 64 * 512 * 256, bytes_accessed=1 << 20, transcendentals=0
        ),
        name="scores",
    )(hidden, queries, lids)


def swap_core(value):
    return lax.ppermute(value, "core", [(0, 1), (1, 0)])


def chip_shift(value, dh, dy):
    pairs = [
        (h * Y + y, ((h + dh) % XH) * Y + (y + dy) % Y) for h in range(XH) for y in range(Y)
    ]
    return lax.ppermute(value, CHIP, pairs)


SHIFTS = [(dh, dy) for dh in range(XH) for dy in range(Y)]


def row_places(sign):
    h, y, core = (lax.axis_index(a) for a in ROW)
    places = []
    for other in (0, 1):
        for dh, dy in SHIFTS:
            places.append(
                lax.rem(h + dh, XH) * (2 * Y)
                + lax.rem(y + Y + sign * dy, Y) * 2
                + (core if other == 0 else 1 - core)
            )
    return jnp.stack(places).astype(jnp.int32)


def gather_row(value):
    mine = [value if s == (0, 0) else chip_shift(value, *s) for s in SHIFTS]
    return mine + [swap_core(v) for v in mine]


def body(
    item_features, self_weight, neighbor_weight, layer_bias, norm_gain, blocks, block_rows,
    block_cols, counts, queries, candidates, positions, position_table, tower_weight,
    score_cotangent,
):
    rows_dev, width = item_features.shape
    tiles, tile_rows, tile_cols = blocks[0, 0], block_rows[0, 0], block_cols[0, 0]
    count = counts[0]
    col_count = lax.axis_size(COL)
    n_row = lax.axis_size(ROW)
    my_row = lax.axis_index(ROW).astype(jnp.int32).reshape(1)

    piece = candidates // rows_dev
    owner = piece // col_count
    local = candidates % rows_dev
    meta = jnp.concatenate(
        [
            (owner * 4 + local // 128).astype(jnp.bfloat16),
            (local % 128).astype(jnp.bfloat16),
            score_cotangent,
            jnp.zeros_like(score_cotangent),
        ],
        axis=1,
    )
    sent = jnp.concatenate([item_features, queries, meta], axis=0)
    gathered = gather_row(sent)
    from_places = row_places(-1)
    weights, lids, all_queries = request_weights(gathered, from_places, my_row, rows_dev)
    natural = jnp.arange(16, dtype=jnp.int32)
    (partial,) = block_products(
        tiles, tile_rows, tile_cols, count, gathered, from_places, rows_dev,
        [col_count * rows_dev], natural, False,
    )
    aggregate = lax.psum_scatter(partial, "z", scatter_dimension=0, tiled=True)
    aggregate = lax.psum_scatter(aggregate, "xl", scatter_dimension=0, tiled=True)

    hidden, back_source, grad_self = layer(
        item_features, aggregate, self_weight, neighbor_weight, layer_bias[None],
        norm_gain[None], weights, all_queries,
    )

    range_source = lax.all_gather(back_source, "xl", axis=0, tiled=True)
    range_source = lax.all_gather(range_source, "z", axis=0, tiled=True)

    raw = lax.psum_scatter(
        owner_scores(hidden, all_queries, lids), ROW, scatter_dimension=0, tiled=True
    )
    tower_values = jnp.sum(jax.nn.relu(position_table) * tower_weight, axis=-1)
    hits = positions[..., None] == jnp.arange(tower_values.shape[0])
    scores = raw * (width**-0.5) + jnp.sum(jnp.where(hits, tower_values, 0.0), axis=-1)

    own, other = block_products(
        tiles, tile_cols, tile_rows, count, [range_source], jnp.zeros((1,), jnp.int32),
        rows_dev * col_count, [8 * rows_dev, 8 * rows_dev], row_places(1), True,
    )
    got = swap_core(other)
    total = grad_self
    for i, s in enumerate(SHIFTS):
        part = slice(i * rows_dev, (i + 1) * rows_dev)
        both = (own[part].astype(jnp.float32) + got[part].astype(jnp.float32)).astype(jnp.bfloat16)
        if s != (0, 0):
            both = chip_shift(both, *s)
        total = total + both.astype(jnp.float32)
    return hidden, scores, total


def solution(mesh):
    split = Mesh(mesh.devices.reshape(2, 4, 2, 8, 2), ALL)
    row, col, both = P(ROW), P(COL), P(ALL, None)
    placed = (
        both, P(), P(), P(), P(),
        P(ROW, COL, None, None, None), P(ROW, COL, None), P(ROW, COL, None), P(ROW, COL),
        both, both, both, P(), P(), both,
    )
    return jax.shard_map(
        body, mesh=split, in_specs=placed, out_specs=(both, both, both), check_vma=False
    )
```

```python
import functools

import jax
import jax.numpy as jnp
from jax import lax
from jax.experimental import pallas as pl
from jax.experimental.pallas import tpu as pltpu
from jax.sharding import Mesh
from jax.sharding import PartitionSpec as P

ROW = ("xh", "y", "core")
COL = ("z", "xl")
ALL = ROW + COL
CHIP = ("xh", "y")
XH, Y, Z = 2, 4, 8
NORM_EPS = 1e-05


def products_kernel(
    n, plan, n_outs, slot_rows, transpose, group, unroll,
    tgt, src, cnt, in_pos, out_pos, blk, *rest,
):
    pieces, rest = rest[:n], rest[n:]
    extra = slot_rows > 512
    if extra:
        ride, rest = rest[0], rest[1:]
    outs, (source, acc, sems) = rest[:n_outs], rest[n_outs:]
    g = pl.program_id(0)

    @pl.when(g == 0)
    def _():
        copies = []
        for i, (which, start, rows) in enumerate(plan):
            at = pl.multiple_of(in_pos[i] * 256, 256)
            copies.append(
                pltpu.make_async_copy(
                    pieces[which].at[pl.ds(start, rows), :],
                    source.at[pl.ds(at, rows), :],
                    sems.at[i],
                )
            )
        for copy in copies:
            copy.start()

        def clear(i, carry):
            at = pl.multiple_of(i * 64, 64)
            acc[pl.ds(at, 64), :] = jnp.zeros((64, acc.shape[1]), jnp.float32)
            return carry

        lax.fori_loop(0, acc.shape[0] // 64, clear, 0)
        for copy in copies:
            copy.wait()

    live = jnp.clip(cnt[0] - g * group, 0, group)
    dims = (((0,), (0,)), ((), ())) if transpose else (((1,), (0,)), ((), ()))

    def one(k):
        s = g * group + k
        to = pl.multiple_of(tgt[s] * 128, 128)
        at = pl.multiple_of(src[s] * 128, 128)
        acc[pl.ds(to, 128), :] += lax.dot_general(
            blk[k], source[pl.ds(at, 128), :], dims, preferred_element_type=jnp.float32
        )

    def some(q, carry):
        for u in range(unroll):
            one(q * unroll + u)
        return carry

    def single(k, carry):
        one(k)
        return carry

    whole = live // unroll
    lax.fori_loop(0, whole, some, 0)
    lax.fori_loop(whole * unroll, live, single, 0)

    @pl.when(g == pl.num_programs(0) - 1)
    def _():
        slot = 0
        for out in outs:
            for i in range(out.shape[0] // slot_rows):

                def store(j, carry, i=i, out=out, slot=slot):
                    to = pl.multiple_of(j * 64, 64)
                    at = pl.multiple_of(out_pos[slot] * 512 + to, 64)
                    out[pl.ds(i * slot_rows + to, 64), :] = acc[pl.ds(at, 64), :].astype(out.dtype)
                    return carry

                lax.fori_loop(0, 8, store, 0)
                if extra:
                    at = pl.multiple_of(out_pos[slot] * 16, 16)
                    to = i * slot_rows + 512
                    out[to : to + 16, :] = ride[pl.ds(at, 16), :]
                slot += 1


def split_pieces(pieces):
    arrays, plan = [], []
    for array, start, rows in pieces:
        which = next((i for i, known in enumerate(arrays) if known is array), len(arrays))
        if which == len(arrays):
            arrays.append(array)
        plan.append((which, start, rows))
    return arrays, tuple(plan)


def block_products(
    tiles, targets, sources, count, pieces, in_pos, out_slots, out_pos, transpose, ride=None,
    group=32, unroll=8,
):
    slots, size, _ = tiles.shape
    arrays, plan = split_pieces(pieces)
    width = arrays[0].shape[1]
    rows = sum(p[2] for p in plan)
    acc_rows = sum(out_slots) * 512
    extra = ride is not None
    slot_rows = 528 if extra else 512

    def tile_map(g, tgt, src, cnt, *_):
        return (jnp.minimum(g, (cnt[0] - 1) // group), 0, 0)

    def whole(g, *_):
        return (0, 0)

    once = pl.Buffered(1)
    return pl.pallas_call(
        functools.partial(
            products_kernel, len(arrays), plan, len(out_slots), slot_rows, transpose, group, unroll
        ),
        out_shape=[
            jax.ShapeDtypeStruct((k * slot_rows, width), jnp.bfloat16) for k in out_slots
        ],
        grid_spec=pltpu.PrefetchScalarGridSpec(
            num_scalar_prefetch=5,
            grid=(slots // group,),
            in_specs=[pl.BlockSpec((group, size, size), tile_map)]
            + [pl.BlockSpec(memory_space=pl.ANY)] * len(arrays)
            + ([pl.BlockSpec(ride.shape, whole, pipeline_mode=once)] if extra else []),
            out_specs=[
                pl.BlockSpec((k * slot_rows, width), whole, pipeline_mode=once) for k in out_slots
            ],
            scratch_shapes=[
                pltpu.VMEM((rows, width), jnp.bfloat16),
                pltpu.VMEM((acc_rows, width), jnp.float32),
                pltpu.SemaphoreType.DMA((len(plan),)),
            ],
        ),
        compiler_params=pltpu.CompilerParams(
            dimension_semantics=("arbitrary",), vmem_limit_bytes=40 << 20
        ),
        cost_estimate=pl.CostEstimate(
            flops=2 * slots * size * size * width,
            bytes_accessed=2 * (slots * size * size + (rows + acc_rows) * width),
            transcendentals=0,
        ),
        name="products",
    )(targets, sources, count, in_pos, out_pos, tiles, *arrays, *([ride] if extra else []))


def weights_kernel(n, plan, in_pos, base, *rest):
    pieces, (weights, lids, queries, packed, sems) = rest[:n], rest[n:]
    copies = []
    for i, (which, start, rows) in enumerate(plan):
        copies.append(
            pltpu.make_async_copy(
                pieces[which].at[pl.ds(start, rows), :], packed.at[in_pos[i]], sems.at[i]
            )
        )
    for copy in copies:
        copy.start()
    for copy in copies:
        copy.wait()
    whole = packed[...]
    queries[...] = whole[:, :16, :].reshape(queries.shape)
    meta = whole[:, 16:, :].reshape(queries.shape).astype(jnp.float32).T
    lid = meta[0:64] * 128.0 + meta[64:128] - base[0].astype(jnp.float32) * 512.0
    cot = meta[128:192]
    lids[0:64, :] = lid
    lids[64:128, :] = cot
    step = 64
    rows = lax.broadcasted_iota(jnp.int32, (step, 256), 0).astype(jnp.float32)

    def chunk(c, carry):
        item = rows + (c * step).astype(jnp.float32)

        def add(k, total):
            return total + jnp.where(
                item == lids[pl.ds(k, 1), :], lids[pl.ds(64 + k, 1), :], 0.0
            )

        total = lax.fori_loop(0, 64, add, jnp.zeros((step, 256), jnp.float32), unroll=4)
        weights[pl.ds(pl.multiple_of(c * step, step), step), :] = total
        return carry

    lax.fori_loop(0, 512 // step, chunk, 0)


def request_weights(pieces, in_pos, my_row):
    arrays, plan = split_pieces(pieces)
    n = len(arrays)
    return pl.pallas_call(
        functools.partial(weights_kernel, n, plan),
        out_shape=[
            jax.ShapeDtypeStruct((512, 256), jnp.float32),
            jax.ShapeDtypeStruct((128, 256), jnp.float32),
            jax.ShapeDtypeStruct((256, 256), jnp.bfloat16),
        ],
        grid_spec=pltpu.PrefetchScalarGridSpec(
            num_scalar_prefetch=2,
            grid=(1,),
            in_specs=[pl.BlockSpec(memory_space=pl.ANY)] * n,
            out_specs=[
                pl.BlockSpec((512, 256), lambda g, *_: (0, 0)),
                pl.BlockSpec((128, 256), lambda g, *_: (0, 0)),
                pl.BlockSpec((256, 256), lambda g, *_: (0, 0)),
            ],
            scratch_shapes=[
                pltpu.VMEM((len(plan), 32, 256), jnp.bfloat16),
                pltpu.SemaphoreType.DMA((len(plan),)),
            ],
        ),
        compiler_params=pltpu.CompilerParams(vmem_limit_bytes=16 << 20),
        cost_estimate=pl.CostEstimate(
            flops=4 * 64 * 512 * 256, bytes_accessed=1 << 20, transcendentals=0
        ),
        name="weights",
    )(in_pos, my_row, *arrays)


def layer_kernel(
    items, agg, self_w, neigh_w, bias, gain, weights, queries, hidden, back, grad_self
):
    pre = jnp.dot(items[...], self_w[...], preferred_element_type=jnp.float32)
    pre = pre + jnp.dot(agg[...], neigh_w[...], preferred_element_type=jnp.float32) + bias[...]
    gate = jax.nn.sigmoid(pre)
    act = pre * gate
    width = act.shape[1]
    inv = lax.rsqrt(jnp.sum(act * act, axis=1, keepdims=True) * (1.0 / width) + NORM_EPS)
    scale = gain[...]
    hidden[...] = (scale * act * inv).astype(hidden.dtype)
    w = weights[...]
    high = w.astype(jnp.bfloat16)
    low = (w - high.astype(jnp.float32)).astype(jnp.bfloat16)
    q = queries[...]
    grad = jnp.dot(high, q, preferred_element_type=jnp.float32)
    grad = grad + jnp.dot(low, q, preferred_element_type=jnp.float32)
    grad = grad * (scale * (width**-0.5))
    mean = jnp.sum(grad * act, axis=1, keepdims=True) * (1.0 / width)
    d_act = inv * (grad - act * (inv * inv * mean))
    d_pre = (d_act * (gate * (1.0 + pre * (1.0 - gate)))).astype(jnp.bfloat16)
    last = (((1,), (1,)), ((), ()))
    back[...] = lax.dot_general(
        d_pre, neigh_w[...], last, preferred_element_type=jnp.float32
    ).astype(back.dtype)
    grad_self[...] = lax.dot_general(d_pre, self_w[...], last, preferred_element_type=jnp.float32)


def layer(items, agg, self_w, neigh_w, bias, gain, weights, queries):
    rows, width = items.shape
    step = 128
    tile = pl.BlockSpec((step, width), lambda g: (g, 0))

    def fixed(shape):
        return pl.BlockSpec(shape, lambda g: (0, 0))

    return pl.pallas_call(
        layer_kernel,
        out_shape=[
            jax.ShapeDtypeStruct((rows, width), jnp.bfloat16),
            jax.ShapeDtypeStruct((rows, width), jnp.bfloat16),
            jax.ShapeDtypeStruct((rows, width), jnp.float32),
        ],
        grid=(rows // step,),
        in_specs=[
            tile, tile, fixed((width, width)), fixed((width, width)), fixed((1, width)),
            fixed((1, width)), tile, fixed((256, width)),
        ],
        out_specs=[tile, tile, tile],
        compiler_params=pltpu.CompilerParams(vmem_limit_bytes=16 << 20),
        cost_estimate=pl.CostEstimate(
            flops=12 * rows * width * width, bytes_accessed=2 << 20, transcendentals=rows * width
        ),
        name="layer",
    )(items, agg, self_w, neigh_w, bias, gain, weights, queries)


def scores_kernel(hidden, queries, lids, out, table, picked):
    table[...] = lax.dot_general(
        hidden[...], queries[...], (((1,), (1,)), ((), ())), preferred_element_type=jnp.float32
    )
    rows = lax.broadcasted_iota(jnp.int32, (8, 256), 0).astype(jnp.float32)

    def pick(k, carry):
        lid = jnp.broadcast_to(lids[pl.ds(k, 1), :], (8, 256)) - rows
        total = jnp.zeros((8, 256), jnp.float32)
        for j in range(64):
            total = total + jnp.where(lid == 8.0 * j, table[8 * j : 8 * j + 8, :], 0.0)
        picked[pl.ds(k, 1), :] = jnp.sum(total, axis=0, keepdims=True)
        return carry

    lax.fori_loop(0, 64, pick, 0)
    value = picked[...].T
    high = value.astype(jnp.bfloat16)
    low = (value - high.astype(jnp.float32)).astype(jnp.bfloat16)
    out[:, 0:64] = high
    out[:, 64:128] = low
    out[:, 128:256] = jnp.zeros((256, 128), jnp.bfloat16)


def owner_scores(hidden, queries, lids):
    return pl.pallas_call(
        scores_kernel,
        out_shape=jax.ShapeDtypeStruct((256, 256), jnp.bfloat16),
        scratch_shapes=[
            pltpu.VMEM((512, 256), jnp.float32),
            pltpu.VMEM((64, 256), jnp.float32),
        ],
        compiler_params=pltpu.CompilerParams(vmem_limit_bytes=16 << 20),
        cost_estimate=pl.CostEstimate(
            flops=4 * 64 * 512 * 256, bytes_accessed=1 << 20, transcendentals=0
        ),
        name="scores",
    )(hidden, queries, lids)


def swap_core(value):
    return lax.ppermute(value, "core", [(0, 1), (1, 0)])


def chip_shift(value, dh, dy):
    pairs = [
        (h * Y + y, ((h + dh) % XH) * Y + (y + dy) % Y) for h in range(XH) for y in range(Y)
    ]
    return lax.ppermute(value, CHIP, pairs)


SHIFTS = [(dh, dy) for dh in range(XH) for dy in range(Y)]


def row_places(sign):
    h, y, core = (lax.axis_index(a) for a in ROW)
    places = []
    for other in (0, 1):
        for dh, dy in SHIFTS:
            places.append(
                lax.rem(h + dh, XH) * (2 * Y)
                + lax.rem(y + Y + sign * dy, Y) * 2
                + (core if other == 0 else 1 - core)
            )
    return jnp.stack(places).astype(jnp.int32)


def gather_row(value):
    rows = value.shape[0]
    mine = [value if s == (0, 0) else chip_shift(value, *s) for s in SHIFTS]
    theirs = swap_core(jnp.concatenate(mine, axis=0))
    return [(v, 0) for v in mine] + [(theirs, i * rows) for i in range(len(mine))]


def reduce_row(own, other):
    got = swap_core(other)
    rows = own.shape[0] // len(SHIFTS)
    parts = []
    for i, s in enumerate(SHIFTS):
        part = slice(i * rows, (i + 1) * rows)
        both = add_up(own[part], got[part])
        parts.append(both if s == (0, 0) else chip_shift(both, *s))
    return parts


def add_up(*parts):
    total = parts[0].astype(jnp.float32)
    for part in parts[1:]:
        total = total + part.astype(jnp.float32)
    return total.astype(jnp.bfloat16)


def z_shift(value, by):
    return lax.ppermute(value, "z", [(i, (i + by) % Z) for i in range(Z)])


def z_shift_by_core(value, sign):
    pairs = []
    for core in (0, 1):
        by = sign if core == 0 else -sign
        pairs += [(core * Z + i, core * Z + (i + by) % Z) for i in range(Z)]
    return lax.ppermute(value, ("core", "z"), pairs)


def swap_x(value):
    return lax.ppermute(value, "xl", [(0, 1), (1, 0)])


NEAR = (0, -1, 1, -2, 2, -3, 3)
RING = NEAR + (4,)


def col_places():
    z, x = lax.axis_index("z"), lax.axis_index("xl")
    return {
        (d, other): lax.rem(z + d + Z, Z) * 2 + (1 - x if other else x)
        for other in (0, 1)
        for d in RING
    }


def gather_col(value):
    first = lax.axis_index("core") == 0
    own, far = {0: value}, {0: swap_x(value)}
    for d in (1, 2):
        for q in (own, far):
            q[-d] = z_shift(q[1 - d], 1)
            q[d] = z_shift(q[d - 1], -1)
    own[-3], own[3] = z_shift(own[-2], 1), z_shift(own[2], -1)
    own[4] = z_shift_by_core(jnp.where(first, own[-3], own[3]), 1)
    for d in (-3, 3, 4):
        far[d] = swap_x(own[d])
    places = col_places()
    pieces = [((own, far)[other][d], 0, value.shape[0]) for d, other in places]
    at = [place * 2 for place in places.values()]
    return pieces, jnp.stack(at).astype(jnp.int32)


def reduce_col(own, far, far3):
    first = lax.axis_index("core") == 0
    rows = own[0].shape[0]
    x4 = swap_x(far[4])
    s1 = add_up(far[1], z_shift(far[2], 1))
    s1m = add_up(far[-1], z_shift(far[-2], -1))
    x3 = swap_x(far3)
    v4 = z_shift_by_core(add_up(own[4], x4), 1)
    zero = jnp.zeros_like(v4)
    s0 = add_up(far[0], z_shift(s1, 1), z_shift(s1m, -1))
    v3 = add_up(own[3], x3[:rows], jnp.where(first, v4, zero))
    v3m = add_up(own[-3], x3[rows:], jnp.where(first, zero, v4))
    across = swap_x(s0)
    v2 = add_up(own[2], z_shift(v3, 1))
    v2m = add_up(own[-2], z_shift(v3m, -1))
    v1 = add_up(own[1], z_shift(v2, 1))
    v1m = add_up(own[-1], z_shift(v2m, -1))
    return add_up(own[0], z_shift(v1, 1), z_shift(v1m, -1), across)


def body(
    item_features, self_weight, neighbor_weight, layer_bias, norm_gain, blocks, block_rows,
    block_cols, counts, queries, candidates, positions, position_table, tower_weight,
    score_cotangent,
):
    rows_dev, width = item_features.shape
    tiles, tile_rows, tile_cols = blocks[0, 0], block_rows[0, 0], block_cols[0, 0]
    count = counts[0]
    col_count = lax.axis_size(COL)
    my_row = lax.axis_index(ROW).astype(jnp.int32).reshape(1)

    piece = candidates // rows_dev
    owner = piece // col_count
    local = candidates % rows_dev
    meta = jnp.concatenate(
        [
            (owner * 4 + local // 128).astype(jnp.bfloat16),
            (local % 128).astype(jnp.bfloat16),
            score_cotangent,
            jnp.zeros_like(score_cotangent),
        ],
        axis=1,
    )
    sent = jnp.concatenate([item_features, queries, meta], axis=0)
    gathered = gather_row(sent)
    from_places = row_places(-1)
    weights, lids, all_queries = request_weights(
        [(v, at + rows_dev, 32) for v, at in gathered], from_places, my_row
    )
    places = col_places()
    keys = [k for k in places if k not in ((3, 1), (-3, 1))]
    order = [places[k] for k in keys] + [places[3, 1], places[-3, 1]]
    partial = block_products(
        tiles, tile_rows, tile_cols, count, [(v, at, rows_dev) for v, at in gathered],
        from_places * 2, [1] * len(keys) + [2], jnp.stack(order).astype(jnp.int32), False,
    )
    own = {d: v for (d, other), v in zip(keys, partial) if not other}
    far = {d: v for (d, other), v in zip(keys, partial) if other}
    aggregate = reduce_col(own, far, partial[-1])

    hidden, back_source, grad_self = layer(
        item_features, aggregate, self_weight, neighbor_weight, layer_bias[None],
        norm_gain[None], weights, all_queries,
    )
    pieces, in_pos = gather_col(back_source)
    ride = owner_scores(hidden, all_queries, lids)
    mine, theirs = block_products(
        tiles, tile_cols, tile_rows, count, pieces, in_pos, [8, 8], row_places(1), True, ride
    )
    total, raw = grad_self, 0.0
    for part in reduce_row(mine, theirs):
        total = total + part[:rows_dev].astype(jnp.float32)
        raw = raw + part[rows_dev:].astype(jnp.float32)
    cands = candidates.shape[1]
    raw = raw[:, :cands] + raw[:, cands : 2 * cands]
    tower_values = jnp.sum(jax.nn.relu(position_table) * tower_weight, axis=-1)
    hits = positions[..., None] == jnp.arange(tower_values.shape[0])
    scores = raw * (width**-0.5) + jnp.sum(jnp.where(hits, tower_values, 0.0), axis=-1)
    return hidden, scores, total


def solution(mesh):
    split = Mesh(mesh.devices.reshape(2, 4, 2, 8, 2), ALL)
    row, col, both = P(ROW), P(COL), P(ALL, None)
    placed = (
        both, P(), P(), P(), P(),
        P(ROW, COL, None, None, None), P(ROW, COL, None), P(ROW, COL, None), P(ROW, COL),
        both, both, both, P(), P(), both,
    )
    return jax.shard_map(
        body, mesh=split, in_specs=placed, out_specs=(both, both, both), check_vma=False
    )
```

```python
import functools

import jax
import jax.numpy as jnp
from jax import lax
from jax.experimental import pallas as pl
from jax.experimental.pallas import tpu as pltpu
from jax.sharding import Mesh
from jax.sharding import PartitionSpec as P

ROW = ("xh", "y", "core")
COL = ("z", "xl")
ALL = ROW + COL
CHIP = ("xh", "y")
XH, Y, Z = 2, 4, 8
NORM_EPS = 1e-05


def products_kernel(
    n, plan, n_outs, slot_rows, transpose, group, unroll,
    tgt, src, cnt, in_pos, out_pos, blk, *rest,
):
    pieces, rest = rest[:n], rest[n:]
    extra = slot_rows > 512
    if extra:
        ride, rest = rest[0], rest[1:]
    outs, (source, acc, sems) = rest[:n_outs], rest[n_outs:]
    g = pl.program_id(0)
    spare = acc.shape[0] // 128 - 1

    @pl.when(g == 0)
    def _():
        copies = []
        for i, (which, start, rows) in enumerate(plan):
            at = pl.multiple_of(in_pos[i] * 256, 256)
            copies.append(
                pltpu.make_async_copy(
                    pieces[which].at[pl.ds(start, rows), :],
                    source.at[pl.ds(at, rows), :],
                    sems.at[i],
                )
            )
        for copy in copies:
            copy.start()

        def clear(i, carry):
            at = pl.multiple_of(i * 64, 64)
            acc[pl.ds(at, 64), :] = jnp.zeros((64, acc.shape[1]), jnp.float32)
            return carry

        lax.fori_loop(0, spare * 2, clear, 0)
        for copy in copies:
            copy.wait()

    live = jnp.clip(cnt[0] - g * group, 0, group)
    dims = (((0,), (0,)), ((), ())) if transpose else (((1,), (0,)), ((), ()))

    def one(k):
        s = g * group + k
        to = pl.multiple_of(jnp.where(s < cnt[0], tgt[s], spare) * 128, 128)
        at = pl.multiple_of(src[s] * 128, 128)
        acc[pl.ds(to, 128), :] += lax.dot_general(
            blk[k], source[pl.ds(at, 128), :], dims, preferred_element_type=jnp.float32
        )

    def some(q, carry):
        for u in range(unroll):
            one(q * unroll + u)
        return carry

    lax.fori_loop(0, (live + unroll - 1) // unroll, some, 0)

    @pl.when(g == pl.num_programs(0) - 1)
    def _():
        slot = 0
        for out in outs:
            for i in range(out.shape[0] // slot_rows):

                def store(j, carry, i=i, out=out, slot=slot):
                    to = pl.multiple_of(j * 64, 64)
                    at = pl.multiple_of(out_pos[slot] * 512 + to, 64)
                    out[pl.ds(i * slot_rows + to, 64), :] = acc[pl.ds(at, 64), :].astype(out.dtype)
                    return carry

                lax.fori_loop(0, 8, store, 0)
                if extra:
                    at = pl.multiple_of(out_pos[slot] * 16, 16)
                    to = i * slot_rows + 512
                    out[to : to + 16, :] = ride[pl.ds(at, 16), :]
                slot += 1


def in_hbm(arrays):
    specs = []
    placed = []
    for a in arrays:
        large = a.shape[0] > 1024
        specs.append(pl.BlockSpec(memory_space=pl.ANY if large else pltpu.MemorySpace.HBM))
        placed.append(
            a if large else pltpu.with_memory_space_constraint(a, pltpu.MemorySpace.HBM)
        )
    return placed, specs


def split_pieces(pieces):
    arrays, plan = [], []
    for array, start, rows in pieces:
        which = next((i for i, known in enumerate(arrays) if known is array), len(arrays))
        if which == len(arrays):
            arrays.append(array)
        plan.append((which, start, rows))
    return arrays, tuple(plan)


def block_products(
    tiles, targets, sources, count, pieces, in_pos, out_slots, out_pos, transpose, ride=None,
    group=32, unroll=16,
):
    slots, size, _ = tiles.shape
    arrays, plan = split_pieces(pieces)
    arrays, specs = in_hbm(arrays)
    width = arrays[0].shape[1]
    rows = sum(p[2] for p in plan)
    acc_rows = sum(out_slots) * 512 + 128
    extra = ride is not None
    slot_rows = 528 if extra else 512

    def tile_map(g, tgt, src, cnt, *_):
        return (jnp.minimum(g, (cnt[0] - 1) // group), 0, 0)

    def whole(g, *_):
        return (0, 0)

    once = pl.Buffered(1)
    return pl.pallas_call(
        functools.partial(
            products_kernel, len(arrays), plan, len(out_slots), slot_rows, transpose, group, unroll
        ),
        out_shape=[
            pltpu.MemorySpace.HBM((k * slot_rows, width), jnp.bfloat16) for k in out_slots
        ],
        grid_spec=pltpu.PrefetchScalarGridSpec(
            num_scalar_prefetch=5,
            grid=(slots // group,),
            in_specs=[pl.BlockSpec((group, size, size), tile_map)]
            + specs
            + ([pl.BlockSpec(ride.shape, whole, pipeline_mode=once)] if extra else []),
            out_specs=[
                pl.BlockSpec((k * slot_rows, width), whole, pipeline_mode=once) for k in out_slots
            ],
            scratch_shapes=[
                pltpu.VMEM((rows, width), jnp.bfloat16),
                pltpu.VMEM((acc_rows, width), jnp.float32),
                pltpu.SemaphoreType.DMA((len(plan),)),
            ],
        ),
        compiler_params=pltpu.CompilerParams(
            dimension_semantics=("arbitrary",), vmem_limit_bytes=22 << 20
        ),
        cost_estimate=pl.CostEstimate(
            flops=2 * slots * size * size * width,
            bytes_accessed=2 * (slots * size * size + (rows + acc_rows) * width),
            transcendentals=0,
        ),
        name="products",
    )(targets, sources, count, in_pos, out_pos, tiles, *arrays, *([ride] if extra else []))


def weights_kernel(n, plan, in_pos, base, *rest):
    pieces, (weights, lids, queries, packed, sems) = rest[:n], rest[n:]
    copies = []
    for i, (which, start, rows) in enumerate(plan):
        copies.append(
            pltpu.make_async_copy(
                pieces[which].at[pl.ds(start, rows), :], packed.at[in_pos[i]], sems.at[i]
            )
        )
    for copy in copies:
        copy.start()
    for copy in copies:
        copy.wait()
    whole = packed[...]
    queries[...] = whole[:, :16, :].reshape(queries.shape)
    meta = whole[:, 16:, :].reshape(queries.shape).astype(jnp.float32).T
    lid = meta[0:64] * 128.0 + meta[64:128] - base[0].astype(jnp.float32) * 512.0
    cot = meta[128:192]
    lids[0:64, :] = lid
    lids[64:128, :] = cot
    step = 64
    rows = lax.broadcasted_iota(jnp.int32, (step, 256), 0).astype(jnp.float32)

    def chunk(c, carry):
        item = rows + (c * step).astype(jnp.float32)

        def add(k, total):
            return total + jnp.where(
                item == lids[pl.ds(k, 1), :], lids[pl.ds(64 + k, 1), :], 0.0
            )

        total = lax.fori_loop(0, 64, add, jnp.zeros((step, 256), jnp.float32), unroll=4)
        weights[pl.ds(pl.multiple_of(c * step, step), step), :] = total
        return carry

    lax.fori_loop(0, 512 // step, chunk, 0)


def request_weights(pieces, in_pos, my_row):
    arrays, plan = split_pieces(pieces)
    arrays, specs = in_hbm(arrays)
    n = len(arrays)
    return pl.pallas_call(
        functools.partial(weights_kernel, n, plan),
        out_shape=[
            jax.ShapeDtypeStruct((512, 256), jnp.float32),
            jax.ShapeDtypeStruct((128, 256), jnp.float32),
            jax.ShapeDtypeStruct((256, 256), jnp.bfloat16),
        ],
        grid_spec=pltpu.PrefetchScalarGridSpec(
            num_scalar_prefetch=2,
            grid=(1,),
            in_specs=specs,
            out_specs=[
                pl.BlockSpec((512, 256), lambda g, *_: (0, 0)),
                pl.BlockSpec((128, 256), lambda g, *_: (0, 0)),
                pl.BlockSpec((256, 256), lambda g, *_: (0, 0)),
            ],
            scratch_shapes=[
                pltpu.VMEM((len(plan), 32, 256), jnp.bfloat16),
                pltpu.SemaphoreType.DMA((len(plan),)),
            ],
        ),
        compiler_params=pltpu.CompilerParams(vmem_limit_bytes=8 << 20),
        cost_estimate=pl.CostEstimate(
            flops=4 * 64 * 512 * 256, bytes_accessed=1 << 20, transcendentals=0
        ),
        name="weights",
    )(in_pos, my_row, *arrays)


def layer_kernel(
    items, agg, self_w, neigh_w, bias, gain, weights, queries, hidden, back, grad_self
):
    pre = jnp.dot(items[...], self_w[...], preferred_element_type=jnp.float32)
    pre = pre + jnp.dot(agg[...], neigh_w[...], preferred_element_type=jnp.float32) + bias[...]
    gate = jax.nn.sigmoid(pre)
    act = pre * gate
    width = act.shape[1]
    inv = lax.rsqrt(jnp.sum(act * act, axis=1, keepdims=True) * (1.0 / width) + NORM_EPS)
    scale = gain[...]
    hidden[...] = (scale * act * inv).astype(hidden.dtype)
    w = weights[...]
    high = w.astype(jnp.bfloat16)
    low = (w - high.astype(jnp.float32)).astype(jnp.bfloat16)
    q = queries[...]
    grad = jnp.dot(high, q, preferred_element_type=jnp.float32)
    grad = grad + jnp.dot(low, q, preferred_element_type=jnp.float32)
    grad = grad * (scale * (width**-0.5))
    mean = jnp.sum(grad * act, axis=1, keepdims=True) * (1.0 / width)
    d_act = inv * (grad - act * (inv * inv * mean))
    d_pre = (d_act * (gate * (1.0 + pre * (1.0 - gate)))).astype(jnp.bfloat16)
    last = (((1,), (1,)), ((), ()))
    back[...] = lax.dot_general(
        d_pre, neigh_w[...], last, preferred_element_type=jnp.float32
    ).astype(back.dtype)
    grad_self[...] = lax.dot_general(d_pre, self_w[...], last, preferred_element_type=jnp.float32)


def layer(items, agg, self_w, neigh_w, bias, gain, weights, queries):
    rows, width = items.shape
    step = 128
    tile = pl.BlockSpec((step, width), lambda g: (g, 0))

    def fixed(shape):
        return pl.BlockSpec(shape, lambda g: (0, 0))

    return pl.pallas_call(
        layer_kernel,
        out_shape=[
            jax.ShapeDtypeStruct((rows, width), jnp.bfloat16),
            jax.ShapeDtypeStruct((rows, width), jnp.bfloat16),
            jax.ShapeDtypeStruct((rows, width), jnp.float32),
        ],
        grid=(rows // step,),
        in_specs=[
            tile, tile, fixed((width, width)), fixed((width, width)), fixed((1, width)),
            fixed((1, width)), tile, fixed((256, width)),
        ],
        out_specs=[tile, tile, tile],
        compiler_params=pltpu.CompilerParams(vmem_limit_bytes=8 << 20),
        cost_estimate=pl.CostEstimate(
            flops=12 * rows * width * width, bytes_accessed=2 << 20, transcendentals=rows * width
        ),
        name="layer",
    )(items, agg, self_w, neigh_w, bias, gain, weights, queries)


def scores_kernel(hidden, queries, lids, out, table, picked):
    table[...] = lax.dot_general(
        hidden[...], queries[...], (((1,), (1,)), ((), ())), preferred_element_type=jnp.float32
    )
    rows = lax.broadcasted_iota(jnp.int32, (8, 256), 0).astype(jnp.float32)

    def pick(k, carry):
        lid = jnp.broadcast_to(lids[pl.ds(k, 1), :], (8, 256)) - rows
        total = jnp.zeros((8, 256), jnp.float32)
        for j in range(64):
            total = total + jnp.where(lid == 8.0 * j, table[8 * j : 8 * j + 8, :], 0.0)
        picked[pl.ds(k, 1), :] = jnp.sum(total, axis=0, keepdims=True)
        return carry

    lax.fori_loop(0, 64, pick, 0)
    value = picked[...].T
    high = value.astype(jnp.bfloat16)
    low = (value - high.astype(jnp.float32)).astype(jnp.bfloat16)
    out[:, 0:64] = high
    out[:, 64:128] = low
    out[:, 128:256] = jnp.zeros((256, 128), jnp.bfloat16)


def owner_scores(hidden, queries, lids):
    return pl.pallas_call(
        scores_kernel,
        out_shape=jax.ShapeDtypeStruct((256, 256), jnp.bfloat16),
        scratch_shapes=[
            pltpu.VMEM((512, 256), jnp.float32),
            pltpu.VMEM((64, 256), jnp.float32),
        ],
        compiler_params=pltpu.CompilerParams(vmem_limit_bytes=8 << 20),
        cost_estimate=pl.CostEstimate(
            flops=4 * 64 * 512 * 256, bytes_accessed=1 << 20, transcendentals=0
        ),
        name="scores",
    )(hidden, queries, lids)


def swap_core(value):
    return lax.ppermute(value, "core", [(0, 1), (1, 0)])


def chip_shift(value, dh, dy):
    pairs = [
        (h * Y + y, ((h + dh) % XH) * Y + (y + dy) % Y) for h in range(XH) for y in range(Y)
    ]
    return lax.ppermute(value, CHIP, pairs)


SHIFTS = [(dh, dy) for dh in range(XH) for dy in range(Y)]


def row_places(sign):
    h, y, core = (lax.axis_index(a) for a in ROW)
    places = []
    for other in (0, 1):
        for dh, dy in SHIFTS:
            places.append(
                lax.rem(h + dh, XH) * (2 * Y)
                + lax.rem(y + Y + sign * dy, Y) * 2
                + (core if other == 0 else 1 - core)
            )
    return jnp.stack(places).astype(jnp.int32)


def gather_row(value):
    rows = value.shape[0]
    mine = [value if s == (0, 0) else chip_shift(value, *s) for s in SHIFTS]
    theirs = swap_core(jnp.concatenate(mine, axis=0))
    return [(v, 0) for v in mine] + [(theirs, i * rows) for i in range(len(mine))]


def reduce_row(own, other):
    got = swap_core(other)
    rows = own.shape[0] // len(SHIFTS)
    parts = []
    for i, s in enumerate(SHIFTS):
        part = slice(i * rows, (i + 1) * rows)
        both = add_up(own[part], got[part])
        parts.append(both if s == (0, 0) else chip_shift(both, *s))
    return parts


def add_up(*parts):
    total = parts[0].astype(jnp.float32)
    for part in parts[1:]:
        total = total + part.astype(jnp.float32)
    return total.astype(jnp.bfloat16)


def z_shift(value, by):
    return lax.ppermute(value, "z", [(i, (i + by) % Z) for i in range(Z)])


def z_shift_by_core(value, sign):
    pairs = []
    for core in (0, 1):
        by = sign if core == 0 else -sign
        pairs += [(core * Z + i, core * Z + (i + by) % Z) for i in range(Z)]
    return lax.ppermute(value, ("core", "z"), pairs)


def swap_x(value):
    return lax.ppermute(value, "xl", [(0, 1), (1, 0)])


NEAR = (0, -1, 1, -2, 2, -3, 3)
RING = NEAR + (4,)


def col_places():
    z, x = lax.axis_index("z"), lax.axis_index("xl")
    return {
        (d, other): lax.rem(z + d + Z, Z) * 2 + (1 - x if other else x)
        for other in (0, 1)
        for d in RING
    }


def gather_col(value, beside):
    first = lax.axis_index("core") == 0
    own, far = {0: value}, {0: swap_x(value)}
    for d in (1, 2):
        if d == 2:
            own[-1], beside = lax.optimization_barrier((own[-1], beside))
        for q in (own, far):
            q[-d] = z_shift(q[1 - d], 1)
            q[d] = z_shift(q[d - 1], -1)
    own[-3], own[3] = z_shift(own[-2], 1), z_shift(own[2], -1)
    own[4] = z_shift_by_core(jnp.where(first, own[-3], own[3]), 1)
    rows = value.shape[0]
    both3 = swap_x(jnp.concatenate([own[-3], own[3]], axis=0))
    far[4] = swap_x(own[4])
    places = col_places()
    pieces = []
    for d, other in places:
        if other and abs(d) == 3:
            pieces.append((both3, 0 if d < 0 else rows, rows))
        else:
            pieces.append(((own, far)[other][d], 0, rows))
    at = [place * 2 for place in places.values()]
    return pieces, jnp.stack(at).astype(jnp.int32), beside


def reduce_col(own, far, far3, beside):
    first = lax.axis_index("core") == 0
    rows = own[0].shape[0]
    x4 = swap_x(far[4])
    own4, beside = lax.optimization_barrier((own[4], beside))
    s1 = add_up(far[1], z_shift(far[2], 1))
    s1m = add_up(far[-1], z_shift(far[-2], -1))
    x3 = swap_x(far3)
    v4 = z_shift_by_core(add_up(own4, x4), 1)
    zero = jnp.zeros_like(v4)
    s0 = add_up(far[0], z_shift(s1, 1), z_shift(s1m, -1))
    v3 = add_up(own[3], x3[:rows], jnp.where(first, v4, zero))
    v3m = add_up(own[-3], x3[rows:], jnp.where(first, zero, v4))
    across = swap_x(s0)
    v2 = add_up(own[2], z_shift(v3, 1))
    v2m = add_up(own[-2], z_shift(v3m, -1))
    v1 = add_up(own[1], z_shift(v2, 1))
    v1m = add_up(own[-1], z_shift(v2m, -1))
    return add_up(own[0], z_shift(v1, 1), z_shift(v1m, -1), across), beside


def body(
    item_features, self_weight, neighbor_weight, layer_bias, norm_gain, blocks, block_rows,
    block_cols, counts, queries, candidates, positions, position_table, tower_weight,
    score_cotangent,
):
    rows_dev, width = item_features.shape
    tiles, tile_rows, tile_cols = blocks[0, 0], block_rows[0, 0], block_cols[0, 0]
    tiles = pltpu.with_memory_space_constraint(tiles, pltpu.MemorySpace.HBM)
    count = counts[0]
    col_count = lax.axis_size(COL)
    my_row = lax.axis_index(ROW).astype(jnp.int32).reshape(1)

    piece = candidates // rows_dev
    owner = piece // col_count
    local = candidates % rows_dev
    meta = jnp.concatenate(
        [
            (owner * 4 + local // 128).astype(jnp.bfloat16),
            (local % 128).astype(jnp.bfloat16),
            score_cotangent,
            jnp.zeros_like(score_cotangent),
        ],
        axis=1,
    )
    sent = jnp.concatenate([item_features, queries, meta], axis=0)
    gathered = gather_row(sent)
    from_places = row_places(-1)
    weights, lids, all_queries = request_weights(
        [(v, at + rows_dev, 32) for v, at in gathered], from_places, my_row
    )
    places = col_places()
    keys = [k for k in places if k not in ((3, 1), (-3, 1))]
    order = [places[k] for k in keys] + [places[3, 1], places[-3, 1]]
    partial = block_products(
        tiles, tile_rows, tile_cols, count, [(v, at, rows_dev) for v, at in gathered],
        from_places * 2, [1] * len(keys) + [2], jnp.stack(order).astype(jnp.int32), False,
    )
    own = {d: v for (d, other), v in zip(keys, partial) if not other}
    far = {d: v for (d, other), v in zip(keys, partial) if other}
    aggregate, (weights, lids, all_queries) = reduce_col(
        own, far, partial[-1], (weights, lids, all_queries)
    )

    hidden, back_source, grad_self = layer(
        item_features, aggregate, self_weight, neighbor_weight, layer_bias[None],
        norm_gain[None], weights, all_queries,
    )
    ride = owner_scores(hidden, all_queries, lids)
    pieces, in_pos, ride = gather_col(back_source, ride)
    mine, theirs = block_products(
        tiles, tile_cols, tile_rows, count, pieces, in_pos, [8, 8], row_places(1), True, ride
    )
    total, raw = grad_self, 0.0
    for part in reduce_row(mine, theirs):
        total = total + part[:rows_dev].astype(jnp.float32)
        raw = raw + part[rows_dev:].astype(jnp.float32)
    cands = candidates.shape[1]
    raw = raw[:, :cands] + raw[:, cands : 2 * cands]
    tower_values = jnp.sum(jax.nn.relu(position_table) * tower_weight, axis=-1)
    hits = positions[..., None] == jnp.arange(tower_values.shape[0])
    scores = raw * (width**-0.5) + jnp.sum(jnp.where(hits, tower_values, 0.0), axis=-1)
    return hidden, scores, total


def solution(mesh):
    split = Mesh(mesh.devices.reshape(2, 4, 2, 8, 2), ALL)
    row, col, both = P(ROW), P(COL), P(ALL, None)
    placed = (
        both, P(), P(), P(), P(),
        P(ROW, COL, None, None, None), P(ROW, COL, None), P(ROW, COL, None), P(ROW, COL),
        both, both, both, P(), P(), both,
    )
    return jax.shard_map(
        body, mesh=split, in_specs=placed, out_specs=(both, both, both), check_vma=False
    )
```

```python
import functools

import jax
import jax.numpy as jnp
from jax import lax
from jax.experimental import pallas as pl
from jax.experimental.pallas import tpu as pltpu
from jax.sharding import Mesh
from jax.sharding import PartitionSpec as P

ROW = ("xh", "y", "core")
COL = ("z", "xl")
ALL = ROW + COL
CHIP = ("xh", "y")
XH, Y, Z = 2, 4, 8
NORM_EPS = 1e-05


def products_kernel(
    n, plan, n_outs, slot_rows, transpose, group, unroll,
    tgt, src, cnt, in_pos, out_pos, blk, *rest,
):
    pieces, rest = rest[:n], rest[n:]
    extra = slot_rows > 512
    if extra:
        ride, rest = rest[0], rest[1:]
    outs, (source, acc, stage, sems, out_sems) = rest[:n_outs], rest[n_outs:]
    g = pl.program_id(0)
    spare = acc.shape[0] // 128 - 1

    @pl.when(g == 0)
    def _():
        copies = []
        for i, (which, start, rows) in enumerate(plan):
            at = pl.multiple_of(in_pos[i] * 256, 256)
            copies.append(
                pltpu.make_async_copy(
                    pieces[which].at[pl.ds(start, rows), :],
                    source.at[pl.ds(at, rows), :],
                    sems.at[i],
                )
            )
        for copy in copies:
            copy.start()

        def clear(i, carry):
            at = pl.multiple_of(i * 128, 128)
            acc[pl.ds(at, 128), :] = jnp.zeros((128, acc.shape[1]), jnp.float32)
            return carry

        lax.fori_loop(0, spare, clear, 0)
        for copy in copies:
            copy.wait()

    live = jnp.clip(cnt[0] - g * group, 0, group)
    dims = (((0,), (0,)), ((), ())) if transpose else (((1,), (0,)), ((), ()))

    def one(k):
        s = g * group + k
        to = pl.multiple_of(jnp.where(s < cnt[0], tgt[s], spare) * 128, 128)
        at = pl.multiple_of(src[s] * 128, 128)
        acc[pl.ds(to, 128), :] += lax.dot_general(
            blk[k], source[pl.ds(at, 128), :], dims, preferred_element_type=jnp.float32
        )

    def some(q, carry):
        for u in range(unroll):
            one(q * unroll + u)
        return carry

    lax.fori_loop(0, (live + unroll - 1) // unroll, some, 0)

    @pl.when(g == pl.num_programs(0) - 1)
    def _():
        slot = 0
        copies = []
        for out in outs:
            for i in range(out.shape[0] // slot_rows):

                def store(j, carry, slot=slot):
                    to = pl.multiple_of(j * 128, 128)
                    at = pl.multiple_of(out_pos[slot] * 512 + to, 128)
                    stage[slot, pl.ds(to, 128), :] = acc[pl.ds(at, 128), :].astype(stage.dtype)
                    return carry

                lax.fori_loop(0, 4, store, 0)
                if extra:
                    at = pl.multiple_of(out_pos[slot] * 16, 16)
                    stage[slot, 512:528, :] = ride[pl.ds(at, 16), :]
                copy = pltpu.make_async_copy(
                    stage.at[slot], out.at[pl.ds(i * slot_rows, slot_rows), :], out_sems.at[slot]
                )
                copy.start()
                copies.append(copy)
                slot += 1
        for copy in copies:
            copy.wait()


def in_hbm(arrays):
    specs = []
    placed = []
    for a in arrays:
        large = a.shape[0] > 1024
        specs.append(pl.BlockSpec(memory_space=pl.ANY if large else pltpu.MemorySpace.HBM))
        placed.append(
            a if large else pltpu.with_memory_space_constraint(a, pltpu.MemorySpace.HBM)
        )
    return placed, specs


def split_pieces(pieces):
    arrays, plan = [], []
    for array, start, rows in pieces:
        which = next((i for i, known in enumerate(arrays) if known is array), len(arrays))
        if which == len(arrays):
            arrays.append(array)
        plan.append((which, start, rows))
    return arrays, tuple(plan)


def block_products(
    tiles, targets, sources, count, pieces, in_pos, out_slots, out_pos, transpose, ride=None,
    group=64, unroll=16,
):
    slots, size, _ = tiles.shape
    arrays, plan = split_pieces(pieces)
    arrays, specs = in_hbm(arrays)
    width = arrays[0].shape[1]
    rows = sum(p[2] for p in plan)
    acc_rows = sum(out_slots) * 512 + 128
    extra = ride is not None
    slot_rows = 528 if extra else 512

    def tile_map(g, tgt, src, cnt, *_):
        return (jnp.minimum(g, (cnt[0] - 1) // group), 0, 0)

    def whole(g, *_):
        return (0, 0)

    once = pl.Buffered(1)
    return pl.pallas_call(
        functools.partial(
            products_kernel, len(arrays), plan, len(out_slots), slot_rows, transpose, group, unroll
        ),
        out_shape=[
            pltpu.MemorySpace.HBM((k * slot_rows, width), jnp.bfloat16) for k in out_slots
        ],
        grid_spec=pltpu.PrefetchScalarGridSpec(
            num_scalar_prefetch=5,
            grid=(slots // group,),
            in_specs=[pl.BlockSpec((group, size, size), tile_map)]
            + specs
            + ([pl.BlockSpec(ride.shape, whole, pipeline_mode=once)] if extra else []),
            out_specs=[pl.BlockSpec(memory_space=pltpu.MemorySpace.HBM)] * len(out_slots),
            scratch_shapes=[
                pltpu.VMEM((rows, width), jnp.bfloat16),
                pltpu.VMEM((acc_rows, width), jnp.float32),
                pltpu.VMEM((sum(out_slots), slot_rows, width), jnp.bfloat16),
                pltpu.SemaphoreType.DMA((len(plan),)),
                pltpu.SemaphoreType.DMA((sum(out_slots),)),
            ],
        ),
        compiler_params=pltpu.CompilerParams(
            dimension_semantics=("arbitrary",), vmem_limit_bytes=22 << 20
        ),
        cost_estimate=pl.CostEstimate(
            flops=2 * slots * size * size * width,
            bytes_accessed=2 * (slots * size * size + (rows + acc_rows) * width),
            transcendentals=0,
        ),
        name="products",
    )(targets, sources, count, in_pos, out_pos, tiles, *arrays, *([ride] if extra else []))


def weights_kernel(n, plan, in_pos, base, *rest):
    pieces, (weights, lids, queries, packed, sems) = rest[:n], rest[n:]
    copies = []
    for i, (which, start, rows) in enumerate(plan):
        copies.append(
            pltpu.make_async_copy(
                pieces[which].at[pl.ds(start, rows), :], packed.at[in_pos[i]], sems.at[i]
            )
        )
    for copy in copies:
        copy.start()
    for copy in copies:
        copy.wait()
    whole = packed[...]
    queries[...] = whole[:, :16, :].reshape(queries.shape)
    meta = whole[:, 16:, :].reshape(queries.shape).astype(jnp.float32).T
    lid = meta[0:64] * 128.0 + meta[64:128] - base[0].astype(jnp.float32) * 512.0
    cot = meta[128:192]
    lids[0:64, :] = lid
    lids[64:128, :] = cot
    step = 64
    rows = lax.broadcasted_iota(jnp.int32, (step, 256), 0).astype(jnp.float32)

    def chunk(c, carry):
        item = rows + (c * step).astype(jnp.float32)

        def add(k, total):
            return total + jnp.where(
                item == lids[pl.ds(k, 1), :], lids[pl.ds(64 + k, 1), :], 0.0
            )

        total = lax.fori_loop(0, 64, add, jnp.zeros((step, 256), jnp.float32), unroll=4)
        weights[pl.ds(pl.multiple_of(c * step, step), step), :] = total
        return carry

    lax.fori_loop(0, 512 // step, chunk, 0)


def request_weights(pieces, in_pos, my_row):
    arrays, plan = split_pieces(pieces)
    arrays, specs = in_hbm(arrays)
    n = len(arrays)
    return pl.pallas_call(
        functools.partial(weights_kernel, n, plan),
        out_shape=[
            jax.ShapeDtypeStruct((512, 256), jnp.float32),
            jax.ShapeDtypeStruct((128, 256), jnp.float32),
            jax.ShapeDtypeStruct((256, 256), jnp.bfloat16),
        ],
        grid_spec=pltpu.PrefetchScalarGridSpec(
            num_scalar_prefetch=2,
            grid=(1,),
            in_specs=specs,
            out_specs=[
                pl.BlockSpec((512, 256), lambda g, *_: (0, 0)),
                pl.BlockSpec((128, 256), lambda g, *_: (0, 0)),
                pl.BlockSpec((256, 256), lambda g, *_: (0, 0)),
            ],
            scratch_shapes=[
                pltpu.VMEM((len(plan), 32, 256), jnp.bfloat16),
                pltpu.SemaphoreType.DMA((len(plan),)),
            ],
        ),
        compiler_params=pltpu.CompilerParams(vmem_limit_bytes=8 << 20),
        cost_estimate=pl.CostEstimate(
            flops=6 * 10**9, bytes_accessed=1 << 20, transcendentals=0
        ),
        name="weights",
    )(in_pos, my_row, *arrays)


def layer_kernel(
    items, agg, self_w, neigh_w, bias, gain, weights, queries, hidden, back, grad_self
):
    pre = jnp.dot(items[...], self_w[...], preferred_element_type=jnp.float32)
    pre = pre + jnp.dot(agg[...], neigh_w[...], preferred_element_type=jnp.float32) + bias[...]
    gate = jax.nn.sigmoid(pre)
    act = pre * gate
    width = act.shape[1]
    inv = lax.rsqrt(jnp.sum(act * act, axis=1, keepdims=True) * (1.0 / width) + NORM_EPS)
    scale = gain[...]
    hidden[...] = (scale * act * inv).astype(hidden.dtype)
    w = weights[...]
    high = w.astype(jnp.bfloat16)
    low = (w - high.astype(jnp.float32)).astype(jnp.bfloat16)
    q = queries[...]
    grad = jnp.dot(high, q, preferred_element_type=jnp.float32)
    grad = grad + jnp.dot(low, q, preferred_element_type=jnp.float32)
    grad = grad * (scale * (width**-0.5))
    mean = jnp.sum(grad * act, axis=1, keepdims=True) * (1.0 / width)
    d_act = inv * (grad - act * (inv * inv * mean))
    d_pre = (d_act * (gate * (1.0 + pre * (1.0 - gate)))).astype(jnp.bfloat16)
    last = (((1,), (1,)), ((), ()))
    back[...] = lax.dot_general(
        d_pre, neigh_w[...], last, preferred_element_type=jnp.float32
    ).astype(back.dtype)
    grad_self[...] = lax.dot_general(d_pre, self_w[...], last, preferred_element_type=jnp.float32)


def layer(items, agg, self_w, neigh_w, bias, gain, weights, queries):
    rows, width = items.shape
    step = 128
    tile = pl.BlockSpec((step, width), lambda g: (g, 0))

    def fixed(shape):
        return pl.BlockSpec(shape, lambda g: (0, 0))

    return pl.pallas_call(
        layer_kernel,
        out_shape=[
            jax.ShapeDtypeStruct((rows, width), jnp.bfloat16),
            jax.ShapeDtypeStruct((rows, width), jnp.bfloat16),
            jax.ShapeDtypeStruct((rows, width), jnp.float32),
        ],
        grid=(rows // step,),
        in_specs=[
            tile, tile, fixed((width, width)), fixed((width, width)), fixed((1, width)),
            fixed((1, width)), tile, fixed((256, width)),
        ],
        out_specs=[tile, tile, tile],
        compiler_params=pltpu.CompilerParams(vmem_limit_bytes=8 << 20),
        cost_estimate=pl.CostEstimate(
            flops=12 * rows * width * width, bytes_accessed=2 << 20, transcendentals=rows * width
        ),
        name="layer",
    )(items, agg, self_w, neigh_w, bias, gain, weights, queries)


def scores_kernel(hidden, queries, lids, out, table, picked):
    table[...] = lax.dot_general(
        hidden[...], queries[...], (((1,), (1,)), ((), ())), preferred_element_type=jnp.float32
    )
    rows = lax.broadcasted_iota(jnp.int32, (8, 256), 0).astype(jnp.float32)

    def pick(k, carry):
        lid = jnp.broadcast_to(lids[pl.ds(k, 1), :], (8, 256)) - rows
        total = jnp.zeros((8, 256), jnp.float32)
        for j in range(64):
            total = total + jnp.where(lid == 8.0 * j, table[8 * j : 8 * j + 8, :], 0.0)
        picked[pl.ds(k, 1), :] = jnp.sum(total, axis=0, keepdims=True)
        return carry

    lax.fori_loop(0, 64, pick, 0)
    value = picked[...].T
    high = value.astype(jnp.bfloat16)
    low = (value - high.astype(jnp.float32)).astype(jnp.bfloat16)
    out[:, 0:64] = high
    out[:, 64:128] = low
    out[:, 128:256] = jnp.zeros((256, 128), jnp.bfloat16)


def owner_scores(hidden, queries, lids):
    return pl.pallas_call(
        scores_kernel,
        out_shape=jax.ShapeDtypeStruct((256, 256), jnp.bfloat16),
        scratch_shapes=[
            pltpu.VMEM((512, 256), jnp.float32),
            pltpu.VMEM((64, 256), jnp.float32),
        ],
        compiler_params=pltpu.CompilerParams(vmem_limit_bytes=8 << 20),
        cost_estimate=pl.CostEstimate(
            flops=6 * 10**9, bytes_accessed=1 << 20, transcendentals=0
        ),
        name="scores",
    )(hidden, queries, lids)


def swap_core(value):
    return lax.ppermute(value, "core", [(0, 1), (1, 0)])


def chip_shift(value, dh, dy):
    pairs = [
        (h * Y + y, ((h + dh) % XH) * Y + (y + dy) % Y) for h in range(XH) for y in range(Y)
    ]
    return lax.ppermute(value, CHIP, pairs)


SHIFTS = [(dh, dy) for dh in range(XH) for dy in range(Y)]


def row_places(sign):
    h, y, core = (lax.axis_index(a) for a in ROW)
    places = []
    for other in (0, 1):
        for dh, dy in SHIFTS:
            places.append(
                lax.rem(h + dh, XH) * (2 * Y)
                + lax.rem(y + Y + sign * dy, Y) * 2
                + (core if other == 0 else 1 - core)
            )
    return jnp.stack(places).astype(jnp.int32)


def gather_row(value):
    rows = value.shape[0]
    mine = [value if s == (0, 0) else chip_shift(value, *s) for s in SHIFTS]
    theirs = swap_core(jnp.concatenate(mine, axis=0))
    return [(v, 0) for v in mine] + [(theirs, i * rows) for i in range(len(mine))]


def reduce_row(own, other):
    got = swap_core(other)
    rows = own.shape[0] // len(SHIFTS)
    parts = []
    for i, s in enumerate(SHIFTS):
        part = slice(i * rows, (i + 1) * rows)
        both = add_up(own[part], got[part])
        parts.append(both if s == (0, 0) else chip_shift(both, *s))
    return parts


def add_up(*parts):
    total = parts[0].astype(jnp.float32)
    for part in parts[1:]:
        total = total + part.astype(jnp.float32)
    return total.astype(jnp.bfloat16)


def z_shift(value, by):
    return lax.ppermute(value, "z", [(i, (i + by) % Z) for i in range(Z)])


def z_shift_by_core(value, sign):
    pairs = []
    for core in (0, 1):
        by = sign if core == 0 else -sign
        pairs += [(core * Z + i, core * Z + (i + by) % Z) for i in range(Z)]
    return lax.ppermute(value, ("core", "z"), pairs)


def swap_x(value):
    return lax.ppermute(value, "xl", [(0, 1), (1, 0)])


NEAR = (0, -1, 1, -2, 2, -3, 3)
RING = NEAR + (4,)


def col_places():
    z, x = lax.axis_index("z"), lax.axis_index("xl")
    return {
        (d, other): lax.rem(z + d + Z, Z) * 2 + (1 - x if other else x)
        for other in (0, 1)
        for d in RING
    }


def gather_col(value, beside):
    first = lax.axis_index("core") == 0
    rows = value.shape[0]
    own, far = {0: value}, {0: swap_x(value)}
    own[-1], own[1] = z_shift(value, 1), z_shift(value, -1)
    own[-1], own[1], far[0], beside = lax.optimization_barrier((own[-1], own[1], far[0], beside))
    own[-2], own[2] = z_shift(own[-1], 1), z_shift(own[1], -1)
    own[-2], own[2], far[0] = lax.optimization_barrier((own[-2], own[2], far[0]))
    own[-3], own[3] = z_shift(own[-2], 1), z_shift(own[2], -1)
    far[-1], far[1] = z_shift(far[0], 1), z_shift(far[0], -1)
    both3 = swap_x(jnp.concatenate([own[-3], own[3]], axis=0))
    own[4] = z_shift_by_core(jnp.where(first, own[-3], own[3]), 1)
    far[-2], far[2] = z_shift(far[-1], 1), z_shift(far[1], -1)
    far[4] = swap_x(own[4])
    places = col_places()
    pieces = []
    for d, other in places:
        if other and abs(d) == 3:
            pieces.append((both3, 0 if d < 0 else rows, rows))
        else:
            pieces.append(((own, far)[other][d], 0, rows))
    at = [place * 2 for place in places.values()]
    return pieces, jnp.stack(at).astype(jnp.int32), beside


def reduce_col(own, far, far3, beside, places):
    first = lax.axis_index("core") == 0
    rows = own[0].shape[0]
    x4, x3 = swap_x(far[4]), swap_x(far3)
    s1 = add_up(far[1], z_shift(far[2], 1))
    s1m = add_up(far[-1], z_shift(far[-2], -1))
    s1, s1m, places = lax.optimization_barrier((s1, s1m, places))
    v4 = z_shift_by_core(add_up(own[4], x4), 1)
    beside = beside(places)
    own2, beside = lax.optimization_barrier((own[2], beside))
    zero = jnp.zeros_like(v4)
    near, near_m = z_shift(s1, 1), z_shift(s1m, -1)
    own3, near, near_m = lax.optimization_barrier((own[3], near, near_m))
    v3 = add_up(own3, x3[:rows], jnp.where(first, v4, zero))
    v3m = add_up(own[-3], x3[rows:], jnp.where(first, zero, v4))
    s0 = add_up(far[0], near, near_m)
    across = swap_x(s0)
    v2 = add_up(own2, z_shift(v3, 1))
    v2m = add_up(own[-2], z_shift(v3m, -1))
    v1 = add_up(own[1], z_shift(v2, 1))
    v1m = add_up(own[-1], z_shift(v2m, -1))
    return add_up(own[0], z_shift(v1, 1), z_shift(v1m, -1), across), beside


def body(
    item_features, self_weight, neighbor_weight, layer_bias, norm_gain, blocks, block_rows,
    block_cols, counts, queries, candidates, positions, position_table, tower_weight,
    score_cotangent,
):
    rows_dev, width = item_features.shape
    tiles, tile_rows, tile_cols = blocks[0, 0], block_rows[0, 0], block_cols[0, 0]
    tiles = pltpu.with_memory_space_constraint(tiles, pltpu.MemorySpace.HBM)
    count = counts[0]
    col_count = lax.axis_size(COL)
    my_row = lax.axis_index(ROW).astype(jnp.int32).reshape(1)

    piece = candidates // rows_dev
    owner = piece // col_count
    local = candidates % rows_dev
    meta = jnp.concatenate(
        [
            (owner * 4 + local // 128).astype(jnp.bfloat16),
            (local % 128).astype(jnp.bfloat16),
            score_cotangent,
            jnp.zeros_like(score_cotangent),
        ],
        axis=1,
    )
    sent = jnp.concatenate([item_features, queries, meta], axis=0)
    gathered = gather_row(sent)
    from_places = row_places(-1)
    places = col_places()
    keys = [k for k in places if k not in ((3, 1), (-3, 1))]
    order = [places[k] for k in keys] + [places[3, 1], places[-3, 1]]
    partial = block_products(
        tiles, tile_rows, tile_cols, count, [(v, at, rows_dev) for v, at in gathered],
        from_places * 2, [1] * len(keys) + [2], jnp.stack(order).astype(jnp.int32), False,
    )
    own = {d: v for (d, other), v in zip(keys, partial) if not other}
    far = {d: v for (d, other), v in zip(keys, partial) if other}
    requests = [(v, at + rows_dev, 32) for v, at in gathered]
    aggregate, (weights, lids, all_queries) = reduce_col(
        own, far, partial[-1], lambda at: request_weights(requests, at, my_row), from_places
    )

    hidden, back_source, grad_self = layer(
        item_features, aggregate, self_weight, neighbor_weight, layer_bias[None],
        norm_gain[None], weights, all_queries,
    )
    ride = owner_scores(hidden, all_queries, lids)
    pieces, in_pos, ride = gather_col(back_source, ride)
    mine, theirs = block_products(
        tiles, tile_cols, tile_rows, count, pieces, in_pos, [8, 8], row_places(1), True, ride
    )
    total, raw = grad_self, 0.0
    for part in reduce_row(mine, theirs):
        total = total + part[:rows_dev].astype(jnp.float32)
        raw = raw + part[rows_dev:].astype(jnp.float32)
    cands = candidates.shape[1]
    raw = raw[:, :cands] + raw[:, cands : 2 * cands]
    tower_values = jnp.sum(jax.nn.relu(position_table) * tower_weight, axis=-1)
    hits = positions[..., None] == jnp.arange(tower_values.shape[0])
    scores = raw * (width**-0.5) + jnp.sum(jnp.where(hits, tower_values, 0.0), axis=-1)
    return hidden, scores, total


def solution(mesh):
    split = Mesh(mesh.devices.reshape(2, 4, 2, 8, 2), ALL)
    row, col, both = P(ROW), P(COL), P(ALL, None)
    placed = (
        both, P(), P(), P(), P(),
        P(ROW, COL, None, None, None), P(ROW, COL, None), P(ROW, COL, None), P(ROW, COL),
        both, both, both, P(), P(), both,
    )
    return jax.shard_map(
        body, mesh=split, in_specs=placed, out_specs=(both, both, both), check_vma=False
    )
```

```python
import functools

import jax
import jax.numpy as jnp
from jax import lax
from jax.experimental import pallas as pl
from jax.experimental.pallas import tpu as pltpu
from jax.sharding import Mesh
from jax.sharding import PartitionSpec as P

ROW = ("xh", "y", "core")
COL = ("z", "xl")
ALL = ROW + COL
CHIP = ("xh", "y")
XH, Y, Z = 2, 4, 8
NORM_EPS = 1e-05


def products_kernel(
    n, plan, n_outs, slot_rows, transpose, group, unroll,
    tgt, src, cnt, in_pos, out_pos, blk, *rest,
):
    pieces, rest = rest[:n], rest[n:]
    extra = slot_rows > 512
    if extra:
        ride, rest = rest[0], rest[1:]
    outs, (source, acc, stage, sems, out_sems) = rest[:n_outs], rest[n_outs:]
    g = pl.program_id(0)
    spare = acc.shape[0] // 128 - 1

    @pl.when(g == 0)
    def _():
        copies = []
        for i, (which, start, rows) in enumerate(plan):
            at = pl.multiple_of(in_pos[i] * 256, 256)
            copies.append(
                pltpu.make_async_copy(
                    pieces[which].at[pl.ds(start, rows), :],
                    source.at[pl.ds(at, rows), :],
                    sems.at[i],
                )
            )
        for copy in copies:
            copy.start()

        def clear(i, carry):
            at = pl.multiple_of(i * 128, 128)
            acc[pl.ds(at, 128), :] = jnp.zeros((128, acc.shape[1]), jnp.float32)
            return carry

        lax.fori_loop(0, spare, clear, 0)
        for copy in copies:
            copy.wait()

    live = jnp.clip(cnt[0] - g * group, 0, group)
    dims = (((0,), (0,)), ((), ())) if transpose else (((1,), (0,)), ((), ()))

    def one(k):
        s = g * group + k
        to = pl.multiple_of(jnp.where(s < cnt[0], tgt[s], spare) * 128, 128)
        at = pl.multiple_of(src[s] * 128, 128)
        acc[pl.ds(to, 128), :] += lax.dot_general(
            blk[k], source[pl.ds(at, 128), :], dims, preferred_element_type=jnp.float32
        )

    def some(q, carry):
        for u in range(unroll):
            one(q * unroll + u)
        return carry

    lax.fori_loop(0, (live + unroll - 1) // unroll, some, 0)

    @pl.when(g == pl.num_programs(0) - 1)
    def _():
        def store(j, carry):
            slot, to = j // 8, pl.multiple_of(lax.rem(j, 8) * 64, 64)
            at = pl.multiple_of(out_pos[slot] * 512 + to, 64)
            stage[slot, pl.ds(to, 64), :] = acc[pl.ds(at, 64), :].astype(stage.dtype)
            return carry

        slot = 0
        copies = []
        for out in outs:
            count = out.shape[0] // slot_rows
            lax.fori_loop(slot * 8, (slot + count) * 8, store, 0)
            for i in range(count):
                if extra:
                    at = pl.multiple_of(out_pos[slot] * 16, 16)
                    stage[slot, 512:528, :] = ride[pl.ds(at, 16), :]
                copy = pltpu.make_async_copy(
                    stage.at[slot], out.at[pl.ds(i * slot_rows, slot_rows), :], out_sems.at[slot]
                )
                copy.start()
                copies.append(copy)
                slot += 1
        for copy in copies:
            copy.wait()


def in_hbm(arrays):
    specs = []
    placed = []
    for a in arrays:
        large = a.shape[0] > 1024
        specs.append(pl.BlockSpec(memory_space=pl.ANY if large else pltpu.MemorySpace.HBM))
        placed.append(
            a if large else pltpu.with_memory_space_constraint(a, pltpu.MemorySpace.HBM)
        )
    return placed, specs


def split_pieces(pieces):
    arrays, plan = [], []
    for array, start, rows in pieces:
        which = next((i for i, known in enumerate(arrays) if known is array), len(arrays))
        if which == len(arrays):
            arrays.append(array)
        plan.append((which, start, rows))
    return arrays, tuple(plan)


def block_products(
    tiles, targets, sources, count, pieces, in_pos, out_slots, out_pos, transpose, ride=None,
    group=64, unroll=16,
):
    slots, size, _ = tiles.shape
    arrays, plan = split_pieces(pieces)
    arrays, specs = in_hbm(arrays)
    width = arrays[0].shape[1]
    rows = sum(p[2] for p in plan)
    acc_rows = sum(out_slots) * 512 + 128
    extra = ride is not None
    slot_rows = 528 if extra else 512

    def tile_map(g, tgt, src, cnt, *_):
        return (jnp.minimum(g, (cnt[0] - 1) // group), 0, 0)

    def whole(g, *_):
        return (0, 0)

    once = pl.Buffered(1)
    return pl.pallas_call(
        functools.partial(
            products_kernel, len(arrays), plan, len(out_slots), slot_rows, transpose, group, unroll
        ),
        out_shape=[
            pltpu.MemorySpace.HBM((k * slot_rows, width), jnp.bfloat16) for k in out_slots
        ],
        grid_spec=pltpu.PrefetchScalarGridSpec(
            num_scalar_prefetch=5,
            grid=(slots // group,),
            in_specs=[pl.BlockSpec((group, size, size), tile_map)]
            + specs
            + ([pl.BlockSpec(ride.shape, whole, pipeline_mode=once)] if extra else []),
            out_specs=[pl.BlockSpec(memory_space=pltpu.MemorySpace.HBM)] * len(out_slots),
            scratch_shapes=[
                pltpu.VMEM((rows, width), jnp.bfloat16),
                pltpu.VMEM((acc_rows, width), jnp.float32),
                pltpu.VMEM((sum(out_slots), slot_rows, width), jnp.bfloat16),
                pltpu.SemaphoreType.DMA((len(plan),)),
                pltpu.SemaphoreType.DMA((sum(out_slots),)),
            ],
        ),
        compiler_params=pltpu.CompilerParams(
            dimension_semantics=("arbitrary",), vmem_limit_bytes=22 << 20
        ),
        cost_estimate=pl.CostEstimate(
            flops=2 * slots * size * size * width,
            bytes_accessed=2 * (slots * size * size + (rows + acc_rows) * width),
            transcendentals=0,
        ),
        name="products",
    )(targets, sources, count, in_pos, out_pos, tiles, *arrays, *([ride] if extra else []))


def weights_kernel(n, plan, in_pos, base, *rest):
    pieces, (weights, lids, queries, packed, sems) = rest[:n], rest[n:]
    copies = []
    for i, (which, start, rows) in enumerate(plan):
        copies.append(
            pltpu.make_async_copy(
                pieces[which].at[pl.ds(start, rows), :], packed.at[in_pos[i]], sems.at[i]
            )
        )
    for copy in copies:
        copy.start()
    for copy in copies:
        copy.wait()
    whole = packed[...]
    queries[...] = whole[:, :16, :].reshape(queries.shape)
    meta = whole[:, 16:, :].reshape(queries.shape).astype(jnp.float32).T
    lid = meta[0:64] * 128.0 + meta[64:128] - base[0].astype(jnp.float32) * 512.0
    cot = meta[128:192]
    lids[0:64, :] = lid
    lids[64:128, :] = cot
    step = 64
    rows = lax.broadcasted_iota(jnp.int32, (step, 256), 0).astype(jnp.float32)

    def chunk(c, carry):
        item = rows + (c * step).astype(jnp.float32)

        def add(k, total):
            return total + jnp.where(
                item == lids[pl.ds(k, 1), :], lids[pl.ds(64 + k, 1), :], 0.0
            )

        total = lax.fori_loop(0, 64, add, jnp.zeros((step, 256), jnp.float32), unroll=4)
        weights[pl.ds(pl.multiple_of(c * step, step), step), :] = total
        return carry

    lax.fori_loop(0, 512 // step, chunk, 0)


def request_weights(pieces, in_pos, my_row):
    arrays, plan = split_pieces(pieces)
    arrays, specs = in_hbm(arrays)
    n = len(arrays)
    return pl.pallas_call(
        functools.partial(weights_kernel, n, plan),
        out_shape=[
            jax.ShapeDtypeStruct((512, 256), jnp.float32),
            jax.ShapeDtypeStruct((128, 256), jnp.float32),
            jax.ShapeDtypeStruct((256, 256), jnp.bfloat16),
        ],
        grid_spec=pltpu.PrefetchScalarGridSpec(
            num_scalar_prefetch=2,
            grid=(1,),
            in_specs=specs,
            out_specs=[
                pl.BlockSpec((512, 256), lambda g, *_: (0, 0)),
                pl.BlockSpec((128, 256), lambda g, *_: (0, 0)),
                pl.BlockSpec((256, 256), lambda g, *_: (0, 0)),
            ],
            scratch_shapes=[
                pltpu.VMEM((len(plan), 32, 256), jnp.bfloat16),
                pltpu.SemaphoreType.DMA((len(plan),)),
            ],
        ),
        compiler_params=pltpu.CompilerParams(vmem_limit_bytes=8 << 20),
        cost_estimate=pl.CostEstimate(
            flops=6 * 10**9, bytes_accessed=1 << 20, transcendentals=0
        ),
        name="weights",
    )(in_pos, my_row, *arrays)


def layer_kernel(
    items, agg, self_w, neigh_w, bias, gain, weights, queries, hidden, back, grad_self
):
    pre = jnp.dot(items[...], self_w[...], preferred_element_type=jnp.float32)
    pre = pre + jnp.dot(agg[...], neigh_w[...], preferred_element_type=jnp.float32) + bias[...]
    gate = jax.nn.sigmoid(pre)
    act = pre * gate
    width = act.shape[1]
    inv = lax.rsqrt(jnp.sum(act * act, axis=1, keepdims=True) * (1.0 / width) + NORM_EPS)
    scale = gain[...]
    hidden[...] = (scale * act * inv).astype(hidden.dtype)
    w = weights[...]
    high = w.astype(jnp.bfloat16)
    low = (w - high.astype(jnp.float32)).astype(jnp.bfloat16)
    q = queries[...]
    grad = jnp.dot(high, q, preferred_element_type=jnp.float32)
    grad = grad + jnp.dot(low, q, preferred_element_type=jnp.float32)
    grad = grad * (scale * (width**-0.5))
    mean = jnp.sum(grad * act, axis=1, keepdims=True) * (1.0 / width)
    d_act = inv * (grad - act * (inv * inv * mean))
    d_pre = (d_act * (gate * (1.0 + pre * (1.0 - gate)))).astype(jnp.bfloat16)
    last = (((1,), (1,)), ((), ()))
    back[...] = lax.dot_general(
        d_pre, neigh_w[...], last, preferred_element_type=jnp.float32
    ).astype(back.dtype)
    grad_self[...] = lax.dot_general(d_pre, self_w[...], last, preferred_element_type=jnp.float32)


def layer(items, agg, self_w, neigh_w, bias, gain, weights, queries):
    rows, width = items.shape
    step = 64
    tile = pl.BlockSpec((step, width), lambda g: (g, 0))

    def fixed(shape):
        return pl.BlockSpec(shape, lambda g: (0, 0))

    return pl.pallas_call(
        layer_kernel,
        out_shape=[
            jax.ShapeDtypeStruct((rows, width), jnp.bfloat16),
            jax.ShapeDtypeStruct((rows, width), jnp.bfloat16),
            jax.ShapeDtypeStruct((rows, width), jnp.float32),
        ],
        grid=(rows // step,),
        in_specs=[
            tile, tile, fixed((width, width)), fixed((width, width)), fixed((1, width)),
            fixed((1, width)), tile, fixed((256, width)),
        ],
        out_specs=[tile, tile, tile],
        compiler_params=pltpu.CompilerParams(vmem_limit_bytes=8 << 20),
        cost_estimate=pl.CostEstimate(
            flops=12 * rows * width * width, bytes_accessed=2 << 20, transcendentals=rows * width
        ),
        name="layer",
    )(items, agg, self_w, neigh_w, bias, gain, weights, queries)


def scores_kernel(hidden, queries, lids, out, table, picked):
    table[...] = lax.dot_general(
        hidden[...], queries[...], (((1,), (1,)), ((), ())), preferred_element_type=jnp.float32
    )
    rows = lax.broadcasted_iota(jnp.int32, (8, 256), 0).astype(jnp.float32)

    def pick(k, carry):
        lid = jnp.broadcast_to(lids[pl.ds(k, 1), :], (8, 256)) - rows
        total = jnp.zeros((8, 256), jnp.float32)
        for j in range(64):
            total = total + jnp.where(lid == 8.0 * j, table[8 * j : 8 * j + 8, :], 0.0)
        picked[pl.ds(k, 1), :] = jnp.sum(total, axis=0, keepdims=True)
        return carry

    lax.fori_loop(0, 64, pick, 0)
    value = picked[...].T
    high = value.astype(jnp.bfloat16)
    low = (value - high.astype(jnp.float32)).astype(jnp.bfloat16)
    out[:, 0:64] = high
    out[:, 64:128] = low
    out[:, 128:256] = jnp.zeros((256, 128), jnp.bfloat16)


def owner_scores(hidden, queries, lids):
    return pl.pallas_call(
        scores_kernel,
        out_shape=jax.ShapeDtypeStruct((256, 256), jnp.bfloat16),
        scratch_shapes=[
            pltpu.VMEM((512, 256), jnp.float32),
            pltpu.VMEM((64, 256), jnp.float32),
        ],
        compiler_params=pltpu.CompilerParams(vmem_limit_bytes=8 << 20),
        cost_estimate=pl.CostEstimate(
            flops=6 * 10**9, bytes_accessed=1 << 20, transcendentals=0
        ),
        name="scores",
    )(hidden, queries, lids)


def swap_core(value):
    return lax.ppermute(value, "core", [(0, 1), (1, 0)])


def chip_shift(value, dh, dy):
    pairs = [
        (h * Y + y, ((h + dh) % XH) * Y + (y + dy) % Y) for h in range(XH) for y in range(Y)
    ]
    return lax.ppermute(value, CHIP, pairs)


def y_shift_by_core(value):
    pairs = []
    for h in range(XH):
        for y in range(Y):
            for core, by in ((0, 1), (1, -1)):
                pairs.append(((h * Y + y) * 2 + core, (h * Y + (y + by) % Y) * 2 + core))
    return lax.ppermute(value, ROW, pairs)


SHIFTS = [(dh, dy) for dh in range(XH) for dy in (0, -1, 1, 2)]


def row_places():
    h, y, core = (lax.axis_index(a) for a in ROW)
    places = []
    for other in (0, 1):
        for dh, dy in SHIFTS:
            places.append(
                lax.rem(h + dh, XH) * (2 * Y)
                + lax.rem(y + Y + dy, Y) * 2
                + (core if other == 0 else 1 - core)
            )
    return jnp.stack(places).astype(jnp.int32)


def join(parts):
    rows, width = parts[0].shape

    def kernel(*refs):
        ins, (out, sems) = refs[: len(parts)], refs[len(parts) :]
        copies = [
            pltpu.make_async_copy(part, out.at[pl.ds(i * rows, rows), :], sems.at[i])
            for i, part in enumerate(ins)
        ]
        for copy in copies:
            copy.start()
        for copy in copies:
            copy.wait()

    return pl.pallas_call(
        kernel,
        out_shape=jax.ShapeDtypeStruct((rows * len(parts), width), parts[0].dtype),
        in_specs=[pl.BlockSpec(memory_space=pltpu.MemorySpace.VMEM)] * len(parts),
        out_specs=pl.BlockSpec(memory_space=pltpu.MemorySpace.HBM),
        scratch_shapes=[pltpu.SemaphoreType.DMA((len(parts),))],
        name="join",
    )(*parts)


def gather_row(value):
    first = lax.axis_index("core") == 0
    rows = value.shape[0]
    across = chip_shift(value, 1, 0)
    mine = {}
    for dh, base in enumerate((value, across)):
        below, above = chip_shift(base, 0, 1), chip_shift(base, 0, -1)
        mine[dh, 0], mine[dh, -1], mine[dh, 1] = base, below, above
        mine[dh, 2] = y_shift_by_core(jnp.where(first, below, above))
    mine = [mine[s] for s in SHIFTS]
    theirs = swap_core(join(mine))
    return [(v, 0) for v in mine] + [(theirs, i * rows) for i in range(len(mine))]


def reduce_row(own, other):
    first = lax.axis_index("core") == 0
    got = swap_core(other)
    rows = own.shape[0] // len(SHIFTS)
    part = {}
    for i, s in enumerate(SHIFTS):
        at = slice(i * rows, (i + 1) * rows)
        part[s] = add_up(own[at], got[at])
    across = None
    for dh in (1, 0):
        far = y_shift_by_core(part[dh, 2])
        zero = jnp.zeros_like(far)
        up = chip_shift(add_up(part[dh, 1], jnp.where(first, far, zero)), 0, 1)
        down = chip_shift(add_up(part[dh, -1], jnp.where(first, zero, far)), 0, -1)
        if dh == 1:
            across = chip_shift(add_up(part[1, 0], up, down), 1, 0)
    return part[0, 0], up, down, across


def add_up(*parts):
    total = parts[0].astype(jnp.float32)
    for part in parts[1:]:
        total = total + part.astype(jnp.float32)
    return total.astype(jnp.bfloat16)


def z_shift(value, by):
    return lax.ppermute(value, "z", [(i, (i + by) % Z) for i in range(Z)])


def z_shift_by_core(value, sign):
    pairs = []
    for core in (0, 1):
        by = sign if core == 0 else -sign
        pairs += [(core * Z + i, core * Z + (i + by) % Z) for i in range(Z)]
    return lax.ppermute(value, ("core", "z"), pairs)


def swap_x(value):
    return lax.ppermute(value, "xl", [(0, 1), (1, 0)])


NEAR = (0, -1, 1, -2, 2, -3, 3)
RING = NEAR + (4,)


def col_places():
    z, x = lax.axis_index("z"), lax.axis_index("xl")
    return {
        (d, other): lax.rem(z + d + Z, Z) * 2 + (1 - x if other else x)
        for other in (0, 1)
        for d in RING
    }


def gather_col(value, beside):
    first = lax.axis_index("core") == 0
    rows = value.shape[0]
    own, far = {0: value}, {0: swap_x(value)}
    own[-1], own[1] = z_shift(value, 1), z_shift(value, -1)
    own[-1], own[1], far[0], beside = lax.optimization_barrier((own[-1], own[1], far[0], beside))
    own[-2], own[2] = z_shift(own[-1], 1), z_shift(own[1], -1)
    own[-2], own[2], far[0] = lax.optimization_barrier((own[-2], own[2], far[0]))
    own[-3], own[3] = z_shift(own[-2], 1), z_shift(own[2], -1)
    far[-1], far[1] = z_shift(far[0], 1), z_shift(far[0], -1)
    both3 = swap_x(jnp.concatenate([own[-3], own[3]], axis=0))
    far[-2], far[2] = z_shift(far[-1], 1), z_shift(far[1], -1)
    nearest = jnp.where(first, own[-3], own[3]), jnp.where(first, both3[:rows], both3[rows:])
    both4 = z_shift_by_core(jnp.concatenate(nearest, axis=0), 1)
    places = col_places()
    pieces = []
    for d, other in places:
        if other and abs(d) == 3:
            pieces.append((both3, 0 if d < 0 else rows, rows))
        elif d == 4:
            pieces.append((both4, other * rows, rows))
        else:
            pieces.append(((own, far)[other][d], 0, rows))
    at = [place * 2 for place in places.values()]
    return pieces, jnp.stack(at).astype(jnp.int32), beside


def reduce_col(own, far, far3, beside, places):
    first = lax.axis_index("core") == 0
    rows = own[0].shape[0]
    x4, x3 = swap_x(far[4]), swap_x(far3)
    s1 = add_up(far[1], z_shift(far[2], 1))
    s1m = add_up(far[-1], z_shift(far[-2], -1))
    s1, s1m, places = lax.optimization_barrier((s1, s1m, places))
    v4 = z_shift_by_core(add_up(own[4], x4), 1)
    beside = beside(places)
    own2, beside = lax.optimization_barrier((own[2], beside))
    zero = jnp.zeros_like(v4)
    near, near_m = z_shift(s1, 1), z_shift(s1m, -1)
    own3, near, near_m = lax.optimization_barrier((own[3], near, near_m))
    v3 = add_up(own3, x3[:rows], jnp.where(first, v4, zero))
    v3m = add_up(own[-3], x3[rows:], jnp.where(first, zero, v4))
    s0 = add_up(far[0], near, near_m)
    across = swap_x(s0)
    v2 = add_up(own2, z_shift(v3, 1))
    v2m = add_up(own[-2], z_shift(v3m, -1))
    v1 = add_up(own[1], z_shift(v2, 1))
    v1m = add_up(own[-1], z_shift(v2m, -1))
    return add_up(own[0], z_shift(v1, 1), z_shift(v1m, -1), across), beside


def body(
    item_features, self_weight, neighbor_weight, layer_bias, norm_gain, blocks, block_rows,
    block_cols, counts, queries, candidates, positions, position_table, tower_weight,
    score_cotangent,
):
    rows_dev, width = item_features.shape
    tiles, tile_rows, tile_cols = blocks[0, 0], block_rows[0, 0], block_cols[0, 0]
    tiles = pltpu.with_memory_space_constraint(tiles, pltpu.MemorySpace.HBM)
    count = counts[0]
    col_count = lax.axis_size(COL)
    my_row = lax.axis_index(ROW).astype(jnp.int32).reshape(1)

    piece = candidates // rows_dev
    owner = piece // col_count
    local = candidates % rows_dev
    meta = jnp.concatenate(
        [
            (owner * 4 + local // 128).astype(jnp.bfloat16),
            (local % 128).astype(jnp.bfloat16),
            score_cotangent,
            jnp.zeros_like(score_cotangent),
        ],
        axis=1,
    )
    sent = jnp.concatenate([item_features, queries, meta], axis=0)
    gathered = gather_row(sent)
    from_places = row_places()
    places = col_places()
    keys = [k for k in places if k not in ((3, 1), (-3, 1))]
    order = [places[k] for k in keys] + [places[3, 1], places[-3, 1]]
    partial = block_products(
        tiles, tile_rows, tile_cols, count, [(v, at, rows_dev) for v, at in gathered],
        from_places * 2, [1] * len(keys) + [2], jnp.stack(order).astype(jnp.int32), False,
    )
    own = {d: v for (d, other), v in zip(keys, partial) if not other}
    far = {d: v for (d, other), v in zip(keys, partial) if other}
    requests = [(v, at + rows_dev, 32) for v, at in gathered]
    aggregate, (weights, lids, all_queries) = reduce_col(
        own, far, partial[-1], lambda at: request_weights(requests, at, my_row), from_places
    )

    hidden, back_source, grad_self = layer(
        item_features, aggregate, self_weight, neighbor_weight, layer_bias[None],
        norm_gain[None], weights, all_queries,
    )
    ride = owner_scores(hidden, all_queries, lids)
    pieces, in_pos, ride = gather_col(back_source, ride)
    mine, theirs = block_products(
        tiles, tile_cols, tile_rows, count, pieces, in_pos, [8, 8], row_places(), True, ride
    )
    total, raw = grad_self, 0.0
    for part in reduce_row(mine, theirs):
        total = total + part[:rows_dev].astype(jnp.float32)
        raw = raw + part[rows_dev:].astype(jnp.float32)
    cands = candidates.shape[1]
    raw = raw[:, :cands] + raw[:, cands : 2 * cands]
    tower_values = jnp.sum(jax.nn.relu(position_table) * tower_weight, axis=-1)
    hits = positions[..., None] == jnp.arange(tower_values.shape[0])
    scores = raw * (width**-0.5) + jnp.sum(jnp.where(hits, tower_values, 0.0), axis=-1)
    return hidden, scores, total


def solution(mesh):
    split = Mesh(mesh.devices.reshape(2, 4, 2, 8, 2), ALL)
    row, col, both = P(ROW), P(COL), P(ALL, None)
    placed = (
        both, P(), P(), P(), P(),
        P(ROW, COL, None, None, None), P(ROW, COL, None), P(ROW, COL, None), P(ROW, COL),
        both, both, both, P(), P(), both,
    )
    return jax.shard_map(
        body, mesh=split, in_specs=placed, out_specs=(both, both, both), check_vma=False
    )
```

```python
import functools

import jax
import jax.numpy as jnp
from jax import lax
from jax.experimental import pallas as pl
from jax.experimental.pallas import tpu as pltpu
from jax.sharding import Mesh
from jax.sharding import PartitionSpec as P

ROW = ("xh", "y", "core")
COL = ("z", "xl")
ALL = ROW + COL
CHIP = ("xh", "y")
XH, Y, Z = 2, 4, 8
NORM_EPS = 1e-05


def products_kernel(
    n, plan, n_outs, slot_rows, transpose, group, unroll,
    tgt, src, cnt, in_pos, out_pos, blk, *rest,
):
    pieces, rest = rest[:n], rest[n:]
    extra = slot_rows > 512
    if extra:
        ride, rest = rest[0], rest[1:]
    outs, (source, acc, stage, sems, out_sems) = rest[:n_outs], rest[n_outs:]
    g = pl.program_id(0)
    spare = acc.shape[0] // 128 - 1

    @pl.when(g == 0)
    def _():
        copies = []
        for i, (which, start, rows) in enumerate(plan):
            at = pl.multiple_of(in_pos[i] * 256, 256)
            copies.append(
                pltpu.make_async_copy(
                    pieces[which].at[pl.ds(start, rows), :],
                    source.at[pl.ds(at, rows), :],
                    sems.at[i],
                )
            )
        for copy in copies:
            copy.start()

        def clear(i, carry):
            at = pl.multiple_of(i * 128, 128)
            acc[pl.ds(at, 128), :] = jnp.zeros((128, acc.shape[1]), jnp.float32)
            return carry

        lax.fori_loop(0, spare, clear, 0)
        for copy in copies:
            copy.wait()

    live = jnp.clip(cnt[0] - g * group, 0, group)
    dims = (((0,), (0,)), ((), ())) if transpose else (((1,), (0,)), ((), ()))

    def one(k):
        s = g * group + k
        to = pl.multiple_of(jnp.where(s < cnt[0], tgt[s], spare) * 128, 128)
        at = pl.multiple_of(src[s] * 128, 128)
        acc[pl.ds(to, 128), :] += lax.dot_general(
            blk[k], source[pl.ds(at, 128), :], dims, preferred_element_type=jnp.float32
        )

    def some(q, carry):
        for u in range(unroll):
            one(q * unroll + u)
        return carry

    lax.fori_loop(0, (live + unroll - 1) // unroll, some, 0)

    @pl.when(g == pl.num_programs(0) - 1)
    def _():
        slot = 0
        copies = []
        for out in outs:
            for i in range(out.shape[0] // slot_rows):

                def store(j, carry, slot=slot):
                    to = pl.multiple_of(j * 128, 128)
                    at = pl.multiple_of(out_pos[slot] * 512 + to, 128)
                    stage[slot, pl.ds(to, 128), :] = acc[pl.ds(at, 128), :].astype(stage.dtype)
                    return carry

                lax.fori_loop(0, 4, store, 0)
                if extra:
                    at = pl.multiple_of(out_pos[slot] * 16, 16)
                    stage[slot, 512:528, :] = ride[pl.ds(at, 16), :]
                copy = pltpu.make_async_copy(
                    stage.at[slot], out.at[pl.ds(i * slot_rows, slot_rows), :], out_sems.at[slot]
                )
                copy.start()
                copies.append(copy)
                slot += 1
        for copy in copies:
            copy.wait()


def in_hbm(arrays):
    specs = []
    placed = []
    for a in arrays:
        large = a.shape[0] > 1024
        specs.append(pl.BlockSpec(memory_space=pl.ANY if large else pltpu.MemorySpace.HBM))
        placed.append(
            a if large else pltpu.with_memory_space_constraint(a, pltpu.MemorySpace.HBM)
        )
    return placed, specs


def split_pieces(pieces):
    arrays, plan = [], []
    for array, start, rows in pieces:
        which = next((i for i, known in enumerate(arrays) if known is array), len(arrays))
        if which == len(arrays):
            arrays.append(array)
        plan.append((which, start, rows))
    return arrays, tuple(plan)


def block_products(
    tiles, targets, sources, count, pieces, in_pos, out_slots, out_pos, transpose, ride=None,
    group=64, unroll=16,
):
    slots, size, _ = tiles.shape
    arrays, plan = split_pieces(pieces)
    arrays, specs = in_hbm(arrays)
    width = arrays[0].shape[1]
    rows = sum(p[2] for p in plan)
    acc_rows = sum(out_slots) * 512 + 128
    extra = ride is not None
    slot_rows = 528 if extra else 512

    def tile_map(g, tgt, src, cnt, *_):
        return (jnp.minimum(g, (cnt[0] - 1) // group), 0, 0)

    def whole(g, *_):
        return (0, 0)

    once = pl.Buffered(1)
    return pl.pallas_call(
        functools.partial(
            products_kernel, len(arrays), plan, len(out_slots), slot_rows, transpose, group, unroll
        ),
        out_shape=[
            pltpu.MemorySpace.HBM((k * slot_rows, width), jnp.bfloat16) for k in out_slots
        ],
        grid_spec=pltpu.PrefetchScalarGridSpec(
            num_scalar_prefetch=5,
            grid=(slots // group,),
            in_specs=[pl.BlockSpec((group, size, size), tile_map)]
            + specs
            + ([pl.BlockSpec(ride.shape, whole, pipeline_mode=once)] if extra else []),
            out_specs=[pl.BlockSpec(memory_space=pltpu.MemorySpace.HBM)] * len(out_slots),
            scratch_shapes=[
                pltpu.VMEM((rows, width), jnp.bfloat16),
                pltpu.VMEM((acc_rows, width), jnp.float32),
                pltpu.VMEM((sum(out_slots), slot_rows, width), jnp.bfloat16),
                pltpu.SemaphoreType.DMA((len(plan),)),
                pltpu.SemaphoreType.DMA((sum(out_slots),)),
            ],
        ),
        compiler_params=pltpu.CompilerParams(
            dimension_semantics=("arbitrary",), vmem_limit_bytes=22 << 20
        ),
        cost_estimate=pl.CostEstimate(
            flops=2 * slots * size * size * width,
            bytes_accessed=2 * (slots * size * size + (rows + acc_rows) * width),
            transcendentals=0,
        ),
        name="products",
    )(targets, sources, count, in_pos, out_pos, tiles, *arrays, *([ride] if extra else []))


def weights_kernel(n, plan, in_pos, base, *rest):
    pieces, (weights, lids, queries, packed, sems) = rest[:n], rest[n:]
    copies = []
    for i, (which, start, rows) in enumerate(plan):
        copies.append(
            pltpu.make_async_copy(
                pieces[which].at[pl.ds(start, rows), :], packed.at[in_pos[i]], sems.at[i]
            )
        )
    for copy in copies:
        copy.start()
    for copy in copies:
        copy.wait()
    whole = packed[...]
    queries[...] = whole[:, :16, :].reshape(queries.shape)
    meta = whole[:, 16:, :].reshape(queries.shape).astype(jnp.float32).T
    lid = meta[0:64] * 128.0 + meta[64:128] - base[0].astype(jnp.float32) * 512.0
    cot = meta[128:192]
    lids[0:64, :] = lid
    lids[64:128, :] = cot
    step = 64
    rows = lax.broadcasted_iota(jnp.int32, (step, 256), 0).astype(jnp.float32)

    def chunk(c, carry):
        item = rows + (c * step).astype(jnp.float32)

        def add(k, total):
            return total + jnp.where(
                item == lids[pl.ds(k, 1), :], lids[pl.ds(64 + k, 1), :], 0.0
            )

        total = lax.fori_loop(0, 64, add, jnp.zeros((step, 256), jnp.float32), unroll=4)
        weights[pl.ds(pl.multiple_of(c * step, step), step), :] = total
        return carry

    lax.fori_loop(0, 512 // step, chunk, 0)


def request_weights(pieces, in_pos, my_row):
    arrays, plan = split_pieces(pieces)
    arrays, specs = in_hbm(arrays)
    n = len(arrays)
    return pl.pallas_call(
        functools.partial(weights_kernel, n, plan),
        out_shape=[
            jax.ShapeDtypeStruct((512, 256), jnp.float32),
            jax.ShapeDtypeStruct((128, 256), jnp.float32),
            jax.ShapeDtypeStruct((256, 256), jnp.bfloat16),
        ],
        grid_spec=pltpu.PrefetchScalarGridSpec(
            num_scalar_prefetch=2,
            grid=(1,),
            in_specs=specs,
            out_specs=[
                pl.BlockSpec((512, 256), lambda g, *_: (0, 0)),
                pl.BlockSpec((128, 256), lambda g, *_: (0, 0)),
                pl.BlockSpec((256, 256), lambda g, *_: (0, 0)),
            ],
            scratch_shapes=[
                pltpu.VMEM((len(plan), 32, 256), jnp.bfloat16),
                pltpu.SemaphoreType.DMA((len(plan),)),
            ],
        ),
        compiler_params=pltpu.CompilerParams(vmem_limit_bytes=8 << 20),
        cost_estimate=pl.CostEstimate(
            flops=6 * 10**9, bytes_accessed=1 << 20, transcendentals=0
        ),
        name="weights",
    )(in_pos, my_row, *arrays)


def layer_kernel(
    items, agg, self_w, neigh_w, bias, gain, weights, queries, hidden, back, grad_self
):
    pre = jnp.dot(items[...], self_w[...], preferred_element_type=jnp.float32)
    pre = pre + jnp.dot(agg[...], neigh_w[...], preferred_element_type=jnp.float32) + bias[...]
    gate = jax.nn.sigmoid(pre)
    act = pre * gate
    width = act.shape[1]
    inv = lax.rsqrt(jnp.sum(act * act, axis=1, keepdims=True) * (1.0 / width) + NORM_EPS)
    scale = gain[...]
    hidden[...] = (scale * act * inv).astype(hidden.dtype)
    w = weights[...]
    high = w.astype(jnp.bfloat16)
    low = (w - high.astype(jnp.float32)).astype(jnp.bfloat16)
    q = queries[...]
    grad = jnp.dot(high, q, preferred_element_type=jnp.float32)
    grad = grad + jnp.dot(low, q, preferred_element_type=jnp.float32)
    grad = grad * (scale * (width**-0.5))
    mean = jnp.sum(grad * act, axis=1, keepdims=True) * (1.0 / width)
    d_act = inv * (grad - act * (inv * inv * mean))
    d_pre = (d_act * (gate * (1.0 + pre * (1.0 - gate)))).astype(jnp.bfloat16)
    last = (((1,), (1,)), ((), ()))
    back[...] = lax.dot_general(
        d_pre, neigh_w[...], last, preferred_element_type=jnp.float32
    ).astype(back.dtype)
    grad_self[...] = lax.dot_general(d_pre, self_w[...], last, preferred_element_type=jnp.float32)


def layer(items, agg, self_w, neigh_w, bias, gain, weights, queries):
    rows, width = items.shape
    step = 128
    tile = pl.BlockSpec((step, width), lambda g: (g, 0))

    def fixed(shape):
        return pl.BlockSpec(shape, lambda g: (0, 0))

    return pl.pallas_call(
        layer_kernel,
        out_shape=[
            jax.ShapeDtypeStruct((rows, width), jnp.bfloat16),
            jax.ShapeDtypeStruct((rows, width), jnp.bfloat16),
            jax.ShapeDtypeStruct((rows, width), jnp.float32),
        ],
        grid=(rows // step,),
        in_specs=[
            tile, tile, fixed((width, width)), fixed((width, width)), fixed((1, width)),
            fixed((1, width)), tile, fixed((256, width)),
        ],
        out_specs=[tile, tile, tile],
        compiler_params=pltpu.CompilerParams(vmem_limit_bytes=8 << 20),
        cost_estimate=pl.CostEstimate(
            flops=12 * rows * width * width, bytes_accessed=2 << 20, transcendentals=rows * width
        ),
        name="layer",
    )(items, agg, self_w, neigh_w, bias, gain, weights, queries)


def scores_kernel(hidden, queries, lids, out, table, picked):
    table[...] = lax.dot_general(
        hidden[...], queries[...], (((1,), (1,)), ((), ())), preferred_element_type=jnp.float32
    )
    rows = lax.broadcasted_iota(jnp.int32, (8, 256), 0).astype(jnp.float32)

    def pick(k, carry):
        lid = jnp.broadcast_to(lids[pl.ds(k, 1), :], (8, 256)) - rows
        total = jnp.zeros((8, 256), jnp.float32)
        for j in range(64):
            total = total + jnp.where(lid == 8.0 * j, table[8 * j : 8 * j + 8, :], 0.0)
        picked[pl.ds(k, 1), :] = jnp.sum(total, axis=0, keepdims=True)
        return carry

    lax.fori_loop(0, 64, pick, 0)
    value = picked[...].T
    high = value.astype(jnp.bfloat16)
    low = (value - high.astype(jnp.float32)).astype(jnp.bfloat16)
    out[:, 0:64] = high
    out[:, 64:128] = low
    out[:, 128:256] = jnp.zeros((256, 128), jnp.bfloat16)


def owner_scores(hidden, queries, lids):
    return pl.pallas_call(
        scores_kernel,
        out_shape=jax.ShapeDtypeStruct((256, 256), jnp.bfloat16),
        scratch_shapes=[
            pltpu.VMEM((512, 256), jnp.float32),
            pltpu.VMEM((64, 256), jnp.float32),
        ],
        compiler_params=pltpu.CompilerParams(vmem_limit_bytes=8 << 20),
        cost_estimate=pl.CostEstimate(
            flops=6 * 10**9, bytes_accessed=1 << 20, transcendentals=0
        ),
        name="scores",
    )(hidden, queries, lids)


def swap_core(value):
    return lax.ppermute(value, "core", [(0, 1), (1, 0)])


def chip_shift(value, dh, dy):
    pairs = [
        (h * Y + y, ((h + dh) % XH) * Y + (y + dy) % Y) for h in range(XH) for y in range(Y)
    ]
    return lax.ppermute(value, CHIP, pairs)


def y_shift_by_core(value):
    pairs = []
    for h in range(XH):
        for y in range(Y):
            for core, by in ((0, 1), (1, -1)):
                pairs.append(((h * Y + y) * 2 + core, (h * Y + (y + by) % Y) * 2 + core))
    return lax.ppermute(value, ROW, pairs)


SHIFTS = [(dh, dy) for dh in range(XH) for dy in (0, -1, 1, 2)]


def row_places():
    h, y, core = (lax.axis_index(a) for a in ROW)
    places = []
    for other in (0, 1):
        for dh, dy in SHIFTS:
            places.append(
                lax.rem(h + dh, XH) * (2 * Y)
                + lax.rem(y + Y + dy, Y) * 2
                + (core if other == 0 else 1 - core)
            )
    return jnp.stack(places).astype(jnp.int32)


def join(parts):
    rows, width = parts[0].shape

    def kernel(*refs):
        ins, (out, sems) = refs[: len(parts)], refs[len(parts) :]
        copies = [
            pltpu.make_async_copy(part, out.at[pl.ds(i * rows, rows), :], sems.at[i])
            for i, part in enumerate(ins)
        ]
        for copy in copies:
            copy.start()
        for copy in copies:
            copy.wait()

    return pl.pallas_call(
        kernel,
        out_shape=jax.ShapeDtypeStruct((rows * len(parts), width), parts[0].dtype),
        in_specs=[pl.BlockSpec(memory_space=pl.ANY)] * len(parts),
        out_specs=pl.BlockSpec(memory_space=pltpu.MemorySpace.HBM),
        scratch_shapes=[pltpu.SemaphoreType.DMA((len(parts),))],
        name="join",
    )(*parts)


def gather_row(value):
    first = lax.axis_index("core") == 0
    rows = value.shape[0]
    across = chip_shift(value, 1, 0)
    mine = {}
    for dh, base in enumerate((value, across)):
        below, above = chip_shift(base, 0, 1), chip_shift(base, 0, -1)
        mine[dh, 0], mine[dh, -1], mine[dh, 1] = base, below, above
        mine[dh, 2] = y_shift_by_core(jnp.where(first, below, above))
    mine = [mine[s] for s in SHIFTS]
    theirs = swap_core(join(mine))
    return [(v, 0) for v in mine] + [(theirs, i * rows) for i in range(len(mine))]


def reduce_row(own, other):
    first = lax.axis_index("core") == 0
    got = swap_core(other)
    rows = own.shape[0] // len(SHIFTS)
    part = {}
    for i, s in enumerate(SHIFTS):
        at = slice(i * rows, (i + 1) * rows)
        part[s] = add_up(own[at], got[at])
    across = None
    both = y_shift_by_core(jnp.concatenate([part[0, 2], part[1, 2]], axis=0))
    for dh in (1, 0):
        far = both[dh * rows : (dh + 1) * rows]
        zero = jnp.zeros_like(far)
        up = chip_shift(add_up(part[dh, 1], jnp.where(first, far, zero)), 0, 1)
        down = chip_shift(add_up(part[dh, -1], jnp.where(first, zero, far)), 0, -1)
        if dh == 1:
            across = chip_shift(add_up(part[1, 0], up, down), 1, 0)
    return part[0, 0], up, down, across


def add_up(*parts):
    total = parts[0].astype(jnp.float32)
    for part in parts[1:]:
        total = total + part.astype(jnp.float32)
    return total.astype(jnp.bfloat16)


def z_shift(value, by):
    return lax.ppermute(value, "z", [(i, (i + by) % Z) for i in range(Z)])


def z_shift_by_core(value, sign):
    pairs = []
    for core in (0, 1):
        by = sign if core == 0 else -sign
        pairs += [(core * Z + i, core * Z + (i + by) % Z) for i in range(Z)]
    return lax.ppermute(value, ("core", "z"), pairs)


def swap_x(value):
    return lax.ppermute(value, "xl", [(0, 1), (1, 0)])


NEAR = (0, -1, 1, -2, 2, -3, 3)
RING = NEAR + (4,)


def col_places():
    z, x = lax.axis_index("z"), lax.axis_index("xl")
    return {
        (d, other): lax.rem(z + d + Z, Z) * 2 + (1 - x if other else x)
        for other in (0, 1)
        for d in RING
    }


def gather_col(value, beside):
    first = lax.axis_index("core") == 0
    rows = value.shape[0]
    own, far = {0: value}, {0: swap_x(value)}
    own[-1], own[1] = z_shift(value, 1), z_shift(value, -1)
    own[-1], own[1], far[0], beside = lax.optimization_barrier((own[-1], own[1], far[0], beside))
    own[-2], own[2] = z_shift(own[-1], 1), z_shift(own[1], -1)
    own[-2], own[2], far[0] = lax.optimization_barrier((own[-2], own[2], far[0]))
    own[-3], own[3] = z_shift(own[-2], 1), z_shift(own[2], -1)
    far[-1], far[1] = z_shift(far[0], 1), z_shift(far[0], -1)
    both3 = swap_x(jnp.concatenate([own[-3], own[3]], axis=0))
    far[-2], far[2] = z_shift(far[-1], 1), z_shift(far[1], -1)
    nearest = jnp.where(first, own[-3], own[3]), jnp.where(first, both3[:rows], both3[rows:])
    both4 = z_shift_by_core(jnp.concatenate(nearest, axis=0), 1)
    places = col_places()
    pieces = []
    for d, other in places:
        if other and abs(d) == 3:
            pieces.append((both3, 0 if d < 0 else rows, rows))
        elif d == 4:
            pieces.append((both4, other * rows, rows))
        else:
            pieces.append(((own, far)[other][d], 0, rows))
    at = [place * 2 for place in places.values()]
    return pieces, jnp.stack(at).astype(jnp.int32), beside


def reduce_col(own, far, far3, beside, places):
    first = lax.axis_index("core") == 0
    rows = own[0].shape[0]
    x4, x3 = swap_x(far[4]), swap_x(far3)
    s1 = add_up(far[1], z_shift(far[2], 1))
    s1m = add_up(far[-1], z_shift(far[-2], -1))
    s1, s1m, places = lax.optimization_barrier((s1, s1m, places))
    v4 = z_shift_by_core(add_up(own[4], x4), 1)
    beside = beside(places)
    own2, beside = lax.optimization_barrier((own[2], beside))
    zero = jnp.zeros_like(v4)
    near, near_m = z_shift(s1, 1), z_shift(s1m, -1)
    own3, near, near_m = lax.optimization_barrier((own[3], near, near_m))
    v3 = add_up(own3, x3[:rows], jnp.where(first, v4, zero))
    v3m = add_up(own[-3], x3[rows:], jnp.where(first, zero, v4))
    s0 = add_up(far[0], near, near_m)
    across = swap_x(s0)
    v2 = add_up(own2, z_shift(v3, 1))
    v2m = add_up(own[-2], z_shift(v3m, -1))
    v1 = add_up(own[1], z_shift(v2, 1))
    v1m = add_up(own[-1], z_shift(v2m, -1))
    return add_up(own[0], z_shift(v1, 1), z_shift(v1m, -1), across), beside


def body(
    item_features, self_weight, neighbor_weight, layer_bias, norm_gain, blocks, block_rows,
    block_cols, counts, queries, candidates, positions, position_table, tower_weight,
    score_cotangent,
):
    rows_dev, width = item_features.shape
    tiles, tile_rows, tile_cols = blocks[0, 0], block_rows[0, 0], block_cols[0, 0]
    tiles = pltpu.with_memory_space_constraint(tiles, pltpu.MemorySpace.HBM)
    count = counts[0]
    col_count = lax.axis_size(COL)
    my_row = lax.axis_index(ROW).astype(jnp.int32).reshape(1)

    piece = candidates // rows_dev
    owner = piece // col_count
    local = candidates % rows_dev
    meta = jnp.concatenate(
        [
            (owner * 4 + local // 128).astype(jnp.bfloat16),
            (local % 128).astype(jnp.bfloat16),
            score_cotangent,
            jnp.zeros_like(score_cotangent),
        ],
        axis=1,
    )
    sent = jnp.concatenate([item_features, queries, meta], axis=0)
    gathered = gather_row(sent)
    from_places = row_places()
    places = col_places()
    keys = [k for k in places if k not in ((3, 1), (-3, 1))]
    order = [places[k] for k in keys] + [places[3, 1], places[-3, 1]]
    partial = block_products(
        tiles, tile_rows, tile_cols, count, [(v, at, rows_dev) for v, at in gathered],
        from_places * 2, [1] * len(keys) + [2], jnp.stack(order).astype(jnp.int32), False,
    )
    own = {d: v for (d, other), v in zip(keys, partial) if not other}
    far = {d: v for (d, other), v in zip(keys, partial) if other}
    requests = [(v, at + rows_dev, 32) for v, at in gathered]
    aggregate, (weights, lids, all_queries) = reduce_col(
        own, far, partial[-1], lambda at: request_weights(requests, at, my_row), from_places
    )

    hidden, back_source, grad_self = layer(
        item_features, aggregate, self_weight, neighbor_weight, layer_bias[None],
        norm_gain[None], weights, all_queries,
    )
    ride = owner_scores(hidden, all_queries, lids)
    pieces, in_pos, ride = gather_col(back_source, ride)
    mine, theirs = block_products(
        tiles, tile_cols, tile_rows, count, pieces, in_pos, [8, 8], row_places(), True, ride
    )
    total, raw = grad_self, 0.0
    for part in reduce_row(mine, theirs):
        total = total + part[:rows_dev].astype(jnp.float32)
        raw = raw + part[rows_dev:].astype(jnp.float32)
    cands = candidates.shape[1]
    raw = raw[:, :cands] + raw[:, cands : 2 * cands]
    tower_values = jnp.sum(jax.nn.relu(position_table) * tower_weight, axis=-1)
    hits = positions[..., None] == jnp.arange(tower_values.shape[0])
    scores = raw * (width**-0.5) + jnp.sum(jnp.where(hits, tower_values, 0.0), axis=-1)
    return hidden, scores, total


def solution(mesh):
    split = Mesh(mesh.devices.reshape(2, 4, 2, 8, 2), ALL)
    row, col, both = P(ROW), P(COL), P(ALL, None)
    placed = (
        both, P(), P(), P(), P(),
        P(ROW, COL, None, None, None), P(ROW, COL, None), P(ROW, COL, None), P(ROW, COL),
        both, both, both, P(), P(), both,
    )
    return jax.shard_map(
        body, mesh=split, in_specs=placed, out_specs=(both, both, both), check_vma=False
    )
```

```python
import functools

import jax
import jax.numpy as jnp
from jax import lax
from jax.experimental import pallas as pl
from jax.experimental.pallas import tpu as pltpu
from jax.sharding import Mesh
from jax.sharding import PartitionSpec as P

ROW = ("xh", "y", "core")
COL = ("z", "xl")
ALL = ROW + COL
CHIP = ("xh", "y")
XH, Y, Z = 2, 4, 8
NORM_EPS = 1e-05


def products_kernel(
    n, plan, n_outs, slot_rows, transpose, group, unroll,
    tgt, src, cnt, in_pos, out_pos, blk, *rest,
):
    pieces, rest = rest[:n], rest[n:]
    extra = slot_rows > 512
    if extra:
        ride, rest = rest[0], rest[1:]
    outs, (source, acc, stage, sems, out_sems) = rest[:n_outs], rest[n_outs:]
    g = pl.program_id(0)
    spare = acc.shape[0] // 128 - 1

    @pl.when(g == 0)
    def _():
        copies = []
        for i, (which, start, rows) in enumerate(plan):
            at = pl.multiple_of(in_pos[i] * 256, 256)
            copies.append(
                pltpu.make_async_copy(
                    pieces[which].at[pl.ds(start, rows), :],
                    source.at[pl.ds(at, rows), :],
                    sems.at[i],
                )
            )
        for copy in copies:
            copy.start()

        def clear(i, carry):
            at = pl.multiple_of(i * 128, 128)
            acc[pl.ds(at, 128), :] = jnp.zeros((128, acc.shape[1]), jnp.float32)
            return carry

        lax.fori_loop(0, spare, clear, 0)
        for copy in copies:
            copy.wait()

    live = jnp.clip(cnt[0] - g * group, 0, group)
    dims = (((0,), (0,)), ((), ())) if transpose else (((1,), (0,)), ((), ()))

    def one(k):
        s = g * group + k
        to = pl.multiple_of(jnp.where(s < cnt[0], tgt[s], spare) * 128, 128)
        at = pl.multiple_of(src[s] * 128, 128)
        acc[pl.ds(to, 128), :] += lax.dot_general(
            blk[k], source[pl.ds(at, 128), :], dims, preferred_element_type=jnp.float32
        )

    def some(q, carry):
        for u in range(unroll):
            one(q * unroll + u)
        return carry

    lax.fori_loop(0, (live + unroll - 1) // unroll, some, 0)

    @pl.when(g == pl.num_programs(0) - 1)
    def _():
        slot = 0
        copies = []
        for out in outs:
            for i in range(out.shape[0] // slot_rows):

                def store(j, carry, slot=slot):
                    to = pl.multiple_of(j * 128, 128)
                    at = pl.multiple_of(out_pos[slot] * 512 + to, 128)
                    stage[slot, pl.ds(to, 128), :] = acc[pl.ds(at, 128), :].astype(stage.dtype)
                    return carry

                lax.fori_loop(0, 4, store, 0)
                if extra:
                    at = pl.multiple_of(out_pos[slot] * 16, 16)
                    stage[slot, 512:528, :] = ride[pl.ds(at, 16), :]
                copy = pltpu.make_async_copy(
                    stage.at[slot], out.at[pl.ds(i * slot_rows, slot_rows), :], out_sems.at[slot]
                )
                copy.start()
                copies.append(copy)
                slot += 1
        for copy in copies:
            copy.wait()


def in_hbm(arrays):
    specs = []
    placed = []
    for a in arrays:
        large = a.shape[0] > 1024
        specs.append(pl.BlockSpec(memory_space=pl.ANY if large else pltpu.MemorySpace.HBM))
        placed.append(
            a if large else pltpu.with_memory_space_constraint(a, pltpu.MemorySpace.HBM)
        )
    return placed, specs


def split_pieces(pieces):
    arrays, plan = [], []
    for array, start, rows in pieces:
        which = next((i for i, known in enumerate(arrays) if known is array), len(arrays))
        if which == len(arrays):
            arrays.append(array)
        plan.append((which, start, rows))
    return arrays, tuple(plan)


def block_products(
    tiles, targets, sources, count, pieces, in_pos, out_slots, out_pos, transpose, ride=None,
    group=64, unroll=16,
):
    slots, size, _ = tiles.shape
    arrays, plan = split_pieces(pieces)
    arrays, specs = in_hbm(arrays)
    width = arrays[0].shape[1]
    rows = sum(p[2] for p in plan)
    acc_rows = sum(out_slots) * 512 + 128
    extra = ride is not None
    slot_rows = 528 if extra else 512

    def tile_map(g, tgt, src, cnt, *_):
        return (jnp.minimum(g, (cnt[0] - 1) // group), 0, 0)

    def whole(g, *_):
        return (0, 0)

    once = pl.Buffered(1)
    return pl.pallas_call(
        functools.partial(
            products_kernel, len(arrays), plan, len(out_slots), slot_rows, transpose, group, unroll
        ),
        out_shape=[
            pltpu.MemorySpace.HBM((k * slot_rows, width), jnp.bfloat16) for k in out_slots
        ],
        grid_spec=pltpu.PrefetchScalarGridSpec(
            num_scalar_prefetch=5,
            grid=(slots // group,),
            in_specs=[pl.BlockSpec((group, size, size), tile_map)]
            + specs
            + ([pl.BlockSpec(ride.shape, whole, pipeline_mode=once)] if extra else []),
            out_specs=[pl.BlockSpec(memory_space=pltpu.MemorySpace.HBM)] * len(out_slots),
            scratch_shapes=[
                pltpu.VMEM((rows, width), jnp.bfloat16),
                pltpu.VMEM((acc_rows, width), jnp.float32),
                pltpu.VMEM((sum(out_slots), slot_rows, width), jnp.bfloat16),
                pltpu.SemaphoreType.DMA((len(plan),)),
                pltpu.SemaphoreType.DMA((sum(out_slots),)),
            ],
        ),
        compiler_params=pltpu.CompilerParams(
            dimension_semantics=("arbitrary",), vmem_limit_bytes=22 << 20
        ),
        cost_estimate=pl.CostEstimate(
            flops=2 * slots * size * size * width,
            bytes_accessed=2 * (slots * size * size + (rows + acc_rows) * width),
            transcendentals=0,
        ),
        name="products",
    )(targets, sources, count, in_pos, out_pos, tiles, *arrays, *([ride] if extra else []))


def weights_kernel(n, plan, in_pos, base, *rest):
    pieces, (weights, lids, queries, packed, sems) = rest[:n], rest[n:]
    copies = []
    for i, (which, start, rows) in enumerate(plan):
        copies.append(
            pltpu.make_async_copy(
                pieces[which].at[pl.ds(start, rows), :], packed.at[in_pos[i]], sems.at[i]
            )
        )
    for copy in copies:
        copy.start()
    for copy in copies:
        copy.wait()
    whole = packed[...]
    queries[...] = whole[:, :16, :].reshape(queries.shape)
    meta = whole[:, 16:, :].reshape(queries.shape).astype(jnp.float32).T
    lid = meta[0:64] * 128.0 + meta[64:128] - base[0].astype(jnp.float32) * 512.0
    cot = meta[128:192]
    lids[0:64, :] = lid
    lids[64:128, :] = cot
    step = 64
    rows = lax.broadcasted_iota(jnp.int32, (step, 256), 0).astype(jnp.float32)

    def chunk(c, carry):
        item = rows + (c * step).astype(jnp.float32)

        def add(k, total):
            return total + jnp.where(
                item == lids[pl.ds(k, 1), :], lids[pl.ds(64 + k, 1), :], 0.0
            )

        total = lax.fori_loop(0, 64, add, jnp.zeros((step, 256), jnp.float32), unroll=4)
        weights[pl.ds(pl.multiple_of(c * step, step), step), :] = total
        return carry

    lax.fori_loop(0, 512 // step, chunk, 0)


def request_weights(pieces, in_pos, my_row):
    arrays, plan = split_pieces(pieces)
    arrays, specs = in_hbm(arrays)
    n = len(arrays)
    return pl.pallas_call(
        functools.partial(weights_kernel, n, plan),
        out_shape=[
            jax.ShapeDtypeStruct((512, 256), jnp.float32),
            jax.ShapeDtypeStruct((128, 256), jnp.float32),
            jax.ShapeDtypeStruct((256, 256), jnp.bfloat16),
        ],
        grid_spec=pltpu.PrefetchScalarGridSpec(
            num_scalar_prefetch=2,
            grid=(1,),
            in_specs=specs,
            out_specs=[
                pl.BlockSpec((512, 256), lambda g, *_: (0, 0)),
                pl.BlockSpec((128, 256), lambda g, *_: (0, 0)),
                pl.BlockSpec((256, 256), lambda g, *_: (0, 0)),
            ],
            scratch_shapes=[
                pltpu.VMEM((len(plan), 32, 256), jnp.bfloat16),
                pltpu.SemaphoreType.DMA((len(plan),)),
            ],
        ),
        compiler_params=pltpu.CompilerParams(vmem_limit_bytes=8 << 20),
        cost_estimate=pl.CostEstimate(
            flops=6 * 10**9, bytes_accessed=1 << 20, transcendentals=0
        ),
        name="weights",
    )(in_pos, my_row, *arrays)


def layer_kernel(
    items, agg, self_w, neigh_w, bias, gain, weights, queries, hidden, back, grad_self
):
    pre = jnp.dot(items[...], self_w[...], preferred_element_type=jnp.float32)
    pre = pre + jnp.dot(agg[...], neigh_w[...], preferred_element_type=jnp.float32) + bias[...]
    gate = jax.nn.sigmoid(pre)
    act = pre * gate
    width = act.shape[1]
    inv = lax.rsqrt(jnp.sum(act * act, axis=1, keepdims=True) * (1.0 / width) + NORM_EPS)
    scale = gain[...]
    hidden[...] = (scale * act * inv).astype(hidden.dtype)
    w = weights[...]
    high = w.astype(jnp.bfloat16)
    low = (w - high.astype(jnp.float32)).astype(jnp.bfloat16)
    q = queries[...]
    grad = jnp.dot(high, q, preferred_element_type=jnp.float32)
    grad = grad + jnp.dot(low, q, preferred_element_type=jnp.float32)
    grad = grad * (scale * (width**-0.5))
    mean = jnp.sum(grad * act, axis=1, keepdims=True) * (1.0 / width)
    d_act = inv * (grad - act * (inv * inv * mean))
    d_pre = (d_act * (gate * (1.0 + pre * (1.0 - gate)))).astype(jnp.bfloat16)
    last = (((1,), (1,)), ((), ()))
    back[...] = lax.dot_general(
        d_pre, neigh_w[...], last, preferred_element_type=jnp.float32
    ).astype(back.dtype)
    grad_self[...] = lax.dot_general(d_pre, self_w[...], last, preferred_element_type=jnp.float32)


def layer(items, agg, self_w, neigh_w, bias, gain, weights, queries):
    rows, width = items.shape
    step = 128
    tile = pl.BlockSpec((step, width), lambda g: (g, 0))

    def fixed(shape):
        return pl.BlockSpec(shape, lambda g: (0, 0))

    return pl.pallas_call(
        layer_kernel,
        out_shape=[
            jax.ShapeDtypeStruct((rows, width), jnp.bfloat16),
            jax.ShapeDtypeStruct((rows, width), jnp.bfloat16),
            jax.ShapeDtypeStruct((rows, width), jnp.float32),
        ],
        grid=(rows // step,),
        in_specs=[
            tile, tile, fixed((width, width)), fixed((width, width)), fixed((1, width)),
            fixed((1, width)), tile, fixed((256, width)),
        ],
        out_specs=[tile, tile, tile],
        compiler_params=pltpu.CompilerParams(vmem_limit_bytes=8 << 20),
        cost_estimate=pl.CostEstimate(
            flops=12 * rows * width * width, bytes_accessed=2 << 20, transcendentals=rows * width
        ),
        name="layer",
    )(items, agg, self_w, neigh_w, bias, gain, weights, queries)


def scores_kernel(hidden, queries, lids, out, table, picked):
    table[...] = lax.dot_general(
        hidden[...], queries[...], (((1,), (1,)), ((), ())), preferred_element_type=jnp.float32
    )
    rows = lax.broadcasted_iota(jnp.int32, (8, 256), 0).astype(jnp.float32)

    def pick(k, carry):
        lid = jnp.broadcast_to(lids[pl.ds(k, 1), :], (8, 256)) - rows
        total = jnp.zeros((8, 256), jnp.float32)
        for j in range(64):
            total = total + jnp.where(lid == 8.0 * j, table[8 * j : 8 * j + 8, :], 0.0)
        picked[pl.ds(k, 1), :] = jnp.sum(total, axis=0, keepdims=True)
        return carry

    lax.fori_loop(0, 64, pick, 0)
    value = picked[...].T
    high = value.astype(jnp.bfloat16)
    low = (value - high.astype(jnp.float32)).astype(jnp.bfloat16)
    out[:, 0:64] = high
    out[:, 64:128] = low
    out[:, 128:256] = jnp.zeros((256, 128), jnp.bfloat16)


def owner_scores(hidden, queries, lids):
    return pl.pallas_call(
        scores_kernel,
        out_shape=jax.ShapeDtypeStruct((256, 256), jnp.bfloat16),
        scratch_shapes=[
            pltpu.VMEM((512, 256), jnp.float32),
            pltpu.VMEM((64, 256), jnp.float32),
        ],
        compiler_params=pltpu.CompilerParams(vmem_limit_bytes=8 << 20),
        cost_estimate=pl.CostEstimate(
            flops=6 * 10**9, bytes_accessed=1 << 20, transcendentals=0
        ),
        name="scores",
    )(hidden, queries, lids)


def swap_core(value):
    return lax.ppermute(value, "core", [(0, 1), (1, 0)])


def chip_shift(value, dh, dy):
    pairs = [
        (h * Y + y, ((h + dh) % XH) * Y + (y + dy) % Y) for h in range(XH) for y in range(Y)
    ]
    return lax.ppermute(value, CHIP, pairs)


def y_shift_by_core(value):
    pairs = []
    for h in range(XH):
        for y in range(Y):
            for core, by in ((0, 1), (1, -1)):
                pairs.append(((h * Y + y) * 2 + core, (h * Y + (y + by) % Y) * 2 + core))
    return lax.ppermute(value, ROW, pairs)


SHIFTS = [(dh, dy) for dh in range(XH) for dy in (0, -1, 1, 2)]


def row_places():
    h, y, core = (lax.axis_index(a) for a in ROW)
    places = []
    for other in (0, 1):
        for dh, dy in SHIFTS:
            places.append(
                lax.rem(h + dh, XH) * (2 * Y)
                + lax.rem(y + Y + dy, Y) * 2
                + (core if other == 0 else 1 - core)
            )
    return jnp.stack(places).astype(jnp.int32)


def gather_row(value):
    first = lax.axis_index("core") == 0
    rows = value.shape[0]
    across = chip_shift(value, 1, 0)
    mine = {}
    for dh, base in enumerate((value, across)):
        below, above = chip_shift(base, 0, 1), chip_shift(base, 0, -1)
        mine[dh, 0], mine[dh, -1], mine[dh, 1] = base, below, above
        mine[dh, 2] = y_shift_by_core(jnp.where(first, below, above))
    mine = [mine[s] for s in SHIFTS]
    theirs = swap_core(jnp.concatenate(mine, axis=0))
    return [(v, 0) for v in mine] + [(theirs, i * rows) for i in range(len(mine))]


def reduce_row(own, other):
    first = lax.axis_index("core") == 0
    got = swap_core(other)
    rows = own.shape[0] // len(SHIFTS)
    part = {}
    for i, s in enumerate(SHIFTS):
        at = slice(i * rows, (i + 1) * rows)
        part[s] = add_up(own[at], got[at])
    across = None
    both = y_shift_by_core(jnp.concatenate([part[0, 2], part[1, 2]], axis=0))
    for dh in (1, 0):
        far = both[dh * rows : (dh + 1) * rows]
        zero = jnp.zeros_like(far)
        up = chip_shift(add_up(part[dh, 1], jnp.where(first, far, zero)), 0, 1)
        down = chip_shift(add_up(part[dh, -1], jnp.where(first, zero, far)), 0, -1)
        if dh == 1:
            across = chip_shift(add_up(part[1, 0], up, down), 1, 0)
    return part[0, 0], up, down, across


def add_up(*parts):
    total = parts[0].astype(jnp.float32)
    for part in parts[1:]:
        total = total + part.astype(jnp.float32)
    return total.astype(jnp.bfloat16)


def z_shift(value, by):
    return lax.ppermute(value, "z", [(i, (i + by) % Z) for i in range(Z)])


def z_shift_by_core(value, sign):
    pairs = []
    for core in (0, 1):
        by = sign if core == 0 else -sign
        pairs += [(core * Z + i, core * Z + (i + by) % Z) for i in range(Z)]
    return lax.ppermute(value, ("core", "z"), pairs)


def swap_x(value):
    return lax.ppermute(value, "xl", [(0, 1), (1, 0)])


NEAR = (0, -1, 1, -2, 2, -3, 3)
RING = NEAR + (4,)


def col_places():
    z, x = lax.axis_index("z"), lax.axis_index("xl")
    return {
        (d, other): lax.rem(z + d + Z, Z) * 2 + (1 - x if other else x)
        for other in (0, 1)
        for d in RING
    }


def gather_col(value, beside):
    first = lax.axis_index("core") == 0
    rows = value.shape[0]
    own, far = {0: value}, {0: swap_x(value)}
    own[-1], own[1] = z_shift(value, 1), z_shift(value, -1)
    own[-1], own[1], far[0], beside = lax.optimization_barrier((own[-1], own[1], far[0], beside))
    own[-2], own[2] = z_shift(own[-1], 1), z_shift(own[1], -1)
    own[-2], own[2], far[0] = lax.optimization_barrier((own[-2], own[2], far[0]))
    own[-3], own[3] = z_shift(own[-2], 1), z_shift(own[2], -1)
    far[-1], far[1] = z_shift(far[0], 1), z_shift(far[0], -1)
    both3 = swap_x(jnp.concatenate([own[-3], own[3]], axis=0))
    far[-2], far[2] = z_shift(far[-1], 1), z_shift(far[1], -1)
    nearest = jnp.where(first, own[-3], own[3]), jnp.where(first, both3[:rows], both3[rows:])
    both4 = z_shift_by_core(jnp.concatenate(nearest, axis=0), 1)
    places = col_places()
    pieces = []
    for d, other in places:
        if other and abs(d) == 3:
            pieces.append((both3, 0 if d < 0 else rows, rows))
        elif d == 4:
            pieces.append((both4, other * rows, rows))
        else:
            pieces.append(((own, far)[other][d], 0, rows))
    at = [place * 2 for place in places.values()]
    return pieces, jnp.stack(at).astype(jnp.int32), beside


def reduce_col(own, far, far3, beside, places):
    first = lax.axis_index("core") == 0
    rows = own[0].shape[0]
    x4, x3 = swap_x(far[4]), swap_x(far3)
    s1 = add_up(far[1], z_shift(far[2], 1))
    s1m = add_up(far[-1], z_shift(far[-2], -1))
    s1, s1m, places = lax.optimization_barrier((s1, s1m, places))
    v4 = z_shift_by_core(add_up(own[4], x4), 1)
    beside = beside(places)
    own2, beside = lax.optimization_barrier((own[2], beside))
    zero = jnp.zeros_like(v4)
    near, near_m = z_shift(s1, 1), z_shift(s1m, -1)
    own3, near, near_m = lax.optimization_barrier((own[3], near, near_m))
    v3 = add_up(own3, x3[:rows], jnp.where(first, v4, zero))
    v3m = add_up(own[-3], x3[rows:], jnp.where(first, zero, v4))
    s0 = add_up(far[0], near, near_m)
    across = swap_x(s0)
    v2 = add_up(own2, z_shift(v3, 1))
    v2m = add_up(own[-2], z_shift(v3m, -1))
    v1 = add_up(own[1], z_shift(v2, 1))
    v1m = add_up(own[-1], z_shift(v2m, -1))
    return add_up(own[0], z_shift(v1, 1), z_shift(v1m, -1), across), beside


def body(
    item_features, self_weight, neighbor_weight, layer_bias, norm_gain, blocks, block_rows,
    block_cols, counts, queries, candidates, positions, position_table, tower_weight,
    score_cotangent,
):
    rows_dev, width = item_features.shape
    tiles, tile_rows, tile_cols = blocks[0, 0], block_rows[0, 0], block_cols[0, 0]
    tiles = pltpu.with_memory_space_constraint(tiles, pltpu.MemorySpace.HBM)
    count = counts[0]
    col_count = lax.axis_size(COL)
    my_row = lax.axis_index(ROW).astype(jnp.int32).reshape(1)

    piece = candidates // rows_dev
    owner = piece // col_count
    local = candidates % rows_dev
    meta = jnp.concatenate(
        [
            (owner * 4 + local // 128).astype(jnp.bfloat16),
            (local % 128).astype(jnp.bfloat16),
            score_cotangent,
            jnp.zeros_like(score_cotangent),
        ],
        axis=1,
    )
    sent = jnp.concatenate([item_features, queries, meta], axis=0)
    gathered = gather_row(sent)
    from_places = row_places()
    places = col_places()
    keys = [k for k in places if k not in ((3, 1), (-3, 1))]
    order = [places[k] for k in keys] + [places[3, 1], places[-3, 1]]
    partial = block_products(
        tiles, tile_rows, tile_cols, count, [(v, at, rows_dev) for v, at in gathered],
        from_places * 2, [1] * len(keys) + [2], jnp.stack(order).astype(jnp.int32), False,
    )
    own = {d: v for (d, other), v in zip(keys, partial) if not other}
    far = {d: v for (d, other), v in zip(keys, partial) if other}
    requests = [(v, at + rows_dev, 32) for v, at in gathered]
    aggregate, (weights, lids, all_queries) = reduce_col(
        own, far, partial[-1], lambda at: request_weights(requests, at, my_row), from_places
    )

    hidden, back_source, grad_self = layer(
        item_features, aggregate, self_weight, neighbor_weight, layer_bias[None],
        norm_gain[None], weights, all_queries,
    )
    ride = owner_scores(hidden, all_queries, lids)
    pieces, in_pos, ride = gather_col(back_source, ride)
    mine, theirs = block_products(
        tiles, tile_cols, tile_rows, count, pieces, in_pos, [8, 8], row_places(), True, ride
    )
    total, raw = grad_self, 0.0
    for part in reduce_row(mine, theirs):
        total = total + part[:rows_dev].astype(jnp.float32)
        raw = raw + part[rows_dev:].astype(jnp.float32)
    cands = candidates.shape[1]
    raw = raw[:, :cands] + raw[:, cands : 2 * cands]
    tower_values = jnp.sum(jax.nn.relu(position_table) * tower_weight, axis=-1)
    hits = positions[..., None] == jnp.arange(tower_values.shape[0])
    scores = raw * (width**-0.5) + jnp.sum(jnp.where(hits, tower_values, 0.0), axis=-1)
    return hidden, scores, total


def solution(mesh):
    split = Mesh(mesh.devices.reshape(2, 4, 2, 8, 2), ALL)
    row, col, both = P(ROW), P(COL), P(ALL, None)
    placed = (
        both, P(), P(), P(), P(),
        P(ROW, COL, None, None, None), P(ROW, COL, None), P(ROW, COL, None), P(ROW, COL),
        both, both, both, P(), P(), both,
    )
    return jax.shard_map(
        body, mesh=split, in_specs=placed, out_specs=(both, both, both), check_vma=False
    )
```
